128 devices in a mesh: shot: 2 (over z_lo), space: 64 (over z_hi, y, x, core).
Axes of the slice: x: 4, y: 4, z: 4 (z_hi: 2, z_lo: 2; z = z_hi * 2 + z_lo), core: 2. Of those that a mesh axis runs over, the one named last changes fastest.
Arguments:
- lame_lambda: float32 [512, 64, 128], P('space'), may hold values from 0.5 to 2
- lame_shear: float32 [512, 64, 128], P('space'), may hold values from 0.2 to 1
- buoyancy: float32 [512, 64, 128], P('space'), may hold values from 0.5 to 1.5
- fwd_state: float32 [9, 4, 512, 64, 128], P(None, 'shot', 'space'), may hold values from -3 to 3
- adj_state: float32 [9, 4, 512, 64, 128], P(None, 'shot', 'space'), may hold values from -3 to 3
- src_index: int32 [4], P('shot'), may hold values from 0 to 4194303
- src_amp: float32 [4, 3], P('shot'), may hold values from -12 to 12
- recv_index: int32 [4, 1024], P('shot'), may hold values from 0 to 4194303
- residual: float32 [4, 3, 1024], P('shot'), may hold values from -12 to 12
Outputs:
- grad_lambda: float32 [512, 64, 128], P('space', 'shot')
- grad_shear: float32 [512, 64, 128], P('space', 'shot')
The draws below stay inside these ranges and needn't reach their ends.
Inputs may be any that keep to these rules, and one draw needn't show every extreme that they name: `src_index`: a cell number (x 64 + y) * 128 + z. `recv_index`: cell numbers (x 64 + y) * 128 + z, repeats possible.
All inputs are finite; a program needn't handle non-finite values.
Results may differ from the reference program's by a relative error of at most 0.00002.
Values sent between devices are 32-bit elements; how exact they have to be, the bound alone decides.
No kernel may reach another device: no remote copies, remote signals or barrier semaphores. Data moves between devices by JAX's collectives and lax.ppermute only.
A program may use at most 320 MiB of HBM per device.

```python
import math
import jax
import jax.numpy as jnp
from jax import lax

NY = 64
NZ = 128
STEPS = 3
RECV = 1024
NX = 512
SHOTS = 4


def plant(entries, stream_key, least, top_value):
    place = [jax.random.randint(jax.random.fold_in(stream_key, axis), (), 0, length) for axis, length in enumerate(entries.shape)]
    longest = entries.shape.index(max(entries.shape))
    next_to = place[:longest] + [(place[longest] + 1) % entries.shape[longest]] + place[longest + 1:]
    return entries.at[tuple(place)].set(least).at[tuple(next_to)].set(top_value)


def shard_levels(stream_key, dims, pieces, smallest, largest):
    loudness = 1.0
    for axis_at, shards_of in pieces:
        heights = jax.random.uniform(jax.random.fold_in(jax.random.fold_in(stream_key, 6), axis_at), (shards_of,), jnp.float32, smallest / len(pieces), largest / len(pieces))
        loudness = loudness * jnp.repeat(jnp.exp(heights), dims[axis_at] // shards_of).reshape((-1,) + (1,) * (len(dims) - 1 - axis_at))
    return loudness


def centred(stream_key, dims, width, bound, shards=(), kind=jnp.bfloat16):
    result = width * jax.random.normal(stream_key, dims, jnp.float32)
    if shards:
        result = result * shard_levels(stream_key, dims, shards, -0.22, 0.18)
    return jnp.clip(result, -bound, bound).astype(kind)


def setup_inputs(seed: int = 0) -> dict:
    keys = jax.random.split(jax.random.key(seed), 10)
    lame_lambda = jnp.clip(jnp.exp(math.log(2.0) - 1.3862944 * jax.random.uniform(keys[0], (NX, NY, NZ), jnp.float32) ** shard_levels(keys[0], (NX, NY, NZ), ((0, 64),), -0.2, 0.2)), 0.5, 2.0)
    lame_shear = jnp.clip(jnp.exp(math.log(1.0) - 1.609438 * jax.random.uniform(keys[1], (NX, NY, NZ), jnp.float32) ** shard_levels(keys[1], (NX, NY, NZ), ((0, 64),), -0.2, 0.2)), 0.2, 1.0)
    buoyancy = jnp.clip(jnp.exp(math.log(1.5) - 1.0986123 * jax.random.uniform(keys[2], (NX, NY, NZ), jnp.float32) ** shard_levels(keys[2], (NX, NY, NZ), ((0, 64),), -0.2, 0.2)), 0.5, 1.5)
    fwd_state = centred(keys[3], (9, SHOTS, NX, NY, NZ), 0.5, 3.0, ((1, 2), (2, 64)), jnp.float32)
    adj_state = centred(keys[4], (9, SHOTS, NX, NY, NZ), 0.5, 3.0, ((1, 2), (2, 64)), jnp.float32)
    src_index = plant(jax.random.randint(keys[5], (SHOTS,), 0, NX * NY * NZ), jax.random.fold_in(keys[5], 1), 0, (NX * NY * NZ) - 1).astype(jnp.int32)
    src_amp = centred(keys[6], (SHOTS, STEPS), 3.0, 12.0, ((0, 2),), jnp.float32)
    recv_index = plant(jax.random.randint(keys[7], (SHOTS, RECV), 0, NX * NY * NZ), jax.random.fold_in(keys[7], 1), 0, (NX * NY * NZ) - 1).astype(jnp.int32)
    residual = centred(keys[8], (SHOTS, STEPS, RECV), 3.0, 12.0, ((0, 2),), jnp.float32)
    return {"lame_lambda": lame_lambda, "lame_shear": lame_shear, "buoyancy": buoyancy, "fwd_state": fwd_state, "adj_state": adj_state, "src_index": src_index, "src_amp": src_amp, "recv_index": recv_index, "residual": residual}


courant = 0.2


def ahead_diff(source, along):
    length = source.shape[along]
    shifted = jnp.concatenate([lax.slice_in_dim(source, 1, length, axis=along), jnp.zeros_like(lax.slice_in_dim(source, 0, 1, axis=along))], axis=along)
    return shifted - source


def behind_diff(source, along):
    length = source.shape[along]
    shifted = jnp.concatenate([jnp.zeros_like(lax.slice_in_dim(source, 0, 1, axis=along)), lax.slice_in_dim(source, 0, length - 1, axis=along)], axis=along)
    return source - shifted


def deposit(source, places, amounts):
    flat_field = source.reshape(-1).at[places].add(amounts)
    return flat_field.reshape(source.shape)


def advance(fields, lame_lambda, lame_shear, buoyancy, factor, vel_push, str_push):
    velocity_x, velocity_y, velocity_z = fields[0], fields[1], fields[2]
    stress_xx, stress_yy, stress_zz = fields[3], fields[4], fields[5]
    stress_yz, stress_xz, stress_xy = fields[6], fields[7], fields[8]
    scaled = factor * buoyancy
    velocity_x = velocity_x + scaled * (ahead_diff(stress_xx, 0) + behind_diff(stress_xy, 1) + behind_diff(stress_xz, 2))
    velocity_y = velocity_y + scaled * (behind_diff(stress_xy, 0) + ahead_diff(stress_yy, 1) + behind_diff(stress_yz, 2))
    velocity_z = velocity_z + scaled * (behind_diff(stress_xz, 0) + behind_diff(stress_yz, 1) + ahead_diff(stress_zz, 2))
    if vel_push is not None:
        velocity_z = deposit(velocity_z, vel_push[0], vel_push[1])
    strain_xx = behind_diff(velocity_x, 0)
    strain_yy = behind_diff(velocity_y, 1)
    strain_zz = behind_diff(velocity_z, 2)
    strain_yz = ahead_diff(velocity_y, 2) + ahead_diff(velocity_z, 1)
    strain_xz = ahead_diff(velocity_x, 2) + ahead_diff(velocity_z, 0)
    strain_xy = ahead_diff(velocity_x, 1) + ahead_diff(velocity_y, 0)
    trace_sum = strain_xx + strain_yy + strain_zz
    bulk_term = lame_lambda * trace_sum
    stress_xx = stress_xx + factor * (bulk_term + 2.0 * lame_shear * strain_xx)
    stress_yy = stress_yy + factor * (bulk_term + 2.0 * lame_shear * strain_yy)
    stress_zz = stress_zz + factor * (bulk_term + 2.0 * lame_shear * strain_zz)
    stress_yz = stress_yz + factor * (lame_shear * strain_yz)
    stress_xz = stress_xz + factor * (lame_shear * strain_xz)
    stress_xy = stress_xy + factor * (lame_shear * strain_xy)
    if str_push is not None:
        stress_xx = deposit(stress_xx, str_push[0], str_push[1])
        stress_yy = deposit(stress_yy, str_push[0], str_push[1])
        stress_zz = deposit(stress_zz, str_push[0], str_push[1])
    fields = jnp.stack([velocity_x, velocity_y, velocity_z, stress_xx, stress_yy, stress_zz, stress_yz, stress_xz, stress_xy])
    strains = jnp.stack([strain_xx, strain_yy, strain_zz, strain_yz, strain_xz, strain_xy])
    return fields, strains


def reference(lame_lambda, lame_shear, buoyancy, fwd_state, adj_state, src_index, src_amp, recv_index, residual):
    grad_lambda = jnp.zeros(lame_lambda.shape, jnp.float32)
    grad_shear = jnp.zeros(lame_lambda.shape, jnp.float32)
    for member in range(SHOTS):
        fields = fwd_state[:, member]
        stored = []
        for moment in range(STEPS):
            push = (src_index[member:member + 1], src_amp[member, moment:moment + 1])
            fields, strain = advance(fields, lame_lambda, lame_shear, buoyancy, courant, None, push)
            stored.append(strain)
        fields = adj_state[:, member]
        for moment in range(STEPS - 1, -1, -1):
            push = (recv_index[member], residual[member, moment])
            fields, strain = advance(fields, lame_lambda, lame_shear, buoyancy, -courant, push, None)
            forward = stored[moment]
            trace_fwd = forward[0] + forward[1] + forward[2]
            trace_adj = strain[0] + strain[1] + strain[2]
            grad_lambda = grad_lambda + trace_fwd * trace_adj
            grad_shear = grad_shear + (2.0 * (forward[0] * strain[0] + forward[1] * strain[1] + forward[2] * strain[2]) + forward[3] * strain[3] + forward[4] * strain[4] + forward[5] * strain[5])
    return grad_lambda, grad_shear
```

```python
import functools

import jax
import jax.numpy as jnp
from jax import lax
from jax.experimental import pallas as pl
from jax.experimental.pallas import tpu as pltpu
from jax.sharding import PartitionSpec as P

courant = 0.2
VX, VY, VZ, SXX, SYY, SZZ, SYZ, SXZ, SXY = range(9)

SLOTS = 14
OWN = 3
PAD = 8

RIGHTWARD = (
    (VX, 5, 3, 0), (VY, 6, 2, 1), (VZ, 6, 2, 1), (SXX, 6, 2, 1), (SYY, 7, 1, 2), (SZZ, 7, 1, 2),
    (SYZ, 7, 1, 2), (SXZ, 6, 2, 1), (SXY, 6, 2, 1),
)
LEFTWARD = (
    (VX, 0, 2, 11), (VY, 0, 3, 11), (VZ, 0, 3, 11), (SXX, 0, 2, 11), (SYY, 0, 2, 11), (SZZ, 0, 2, 11),
    (SYZ, 0, 2, 11), (SXZ, 0, 2, 11), (SXY, 0, 2, 11),
)
MATS_RIGHTWARD = (6, 1)
MATS_LEFTWARD = (0, 11)
SENT = 20
CHUNK = 32


def lanes(rows):
    return lax.broadcasted_iota(jnp.int32, (rows, 128), 1)


def below_z(x):
    return jnp.where(lanes(x.shape[0]) == 0, 0.0, pltpu.roll(x, 1, 1))


def above_z(x):
    return jnp.where(lanes(x.shape[0]) == 127, 0.0, pltpu.roll(x, 127, 1))


def velocity_plane(w, kb, q, inject=None):
    for start in range(0, 64, CHUNK):
        at = pl.ds(PAD + start, CHUNK)
        down = pl.ds(PAD + start - 1, CHUNK)
        up = pl.ds(PAD + start + 1, CHUNK)
        flat = pl.ds(start, CHUNK)
        xy_b, xz_b = w[SXY, q - 1, at, :], w[SXZ, q - 1, at, :]
        w[VX, q - 1, at, :] += kb(q - 1, flat) * (
            (w[SXX, q, at, :] - w[SXX, q - 1, at, :])
            + (xy_b - w[SXY, q - 1, down, :])
            + (xz_b - below_z(xz_b))
        )
        yz, zz = w[SYZ, q, at, :], w[SZZ, q, at, :]
        scaled = kb(q, flat)
        w[VY, q, at, :] += scaled * (
            (w[SXY, q, at, :] - xy_b) + (w[SYY, q, up, :] - w[SYY, q, at, :]) + (yz - below_z(yz))
        )
        new_z = w[VZ, q, at, :] + scaled * (
            (w[SXZ, q, at, :] - xz_b) + (yz - w[SYZ, q, down, :]) + (above_z(zz) - zz)
        )
        if inject is not None:
            new_z = new_z + inject[q, flat, :]
        w[VZ, q, at, :] = new_z


def strain_chunk(w, q, start):
    at = pl.ds(PAD + start, CHUNK)
    down = pl.ds(PAD + start - 1, CHUNK)
    up = pl.ds(PAD + start + 1, CHUNK)
    vx, vy, vz = w[VX, q, at, :], w[VY, q, at, :], w[VZ, q, at, :]
    exx = vx - w[VX, q - 1, at, :]
    eyy = vy - w[VY, q, down, :]
    ezz = vz - below_z(vz)
    eyz = (above_z(vy) - vy) + (w[VZ, q, up, :] - vz)
    exz = (above_z(vx) - vx) + (w[VZ, q + 1, at, :] - vz)
    exy = (w[VX, q, up, :] - vx) + (w[VY, q + 1, at, :] - vy)
    return exx, eyy, ezz, eyz, exz, exy


def stress_chunk(w, mats, q, start, strain):
    at = pl.ds(PAD + start, CHUNK)
    flat = pl.ds(start, CHUNK)
    exx, eyy, ezz, eyz, exz, exy = strain
    twice = mats[2, q, flat, :]
    bulk = mats[1, q, flat, :] * (exx + eyy + ezz)
    once = 0.5 * twice
    w[SXX, q, at, :] += bulk + twice * exx
    w[SYY, q, at, :] += bulk + twice * eyy
    w[SZZ, q, at, :] += bulk + twice * ezz
    w[SYZ, q, at, :] += once * eyz
    w[SXZ, q, at, :] += once * exz
    w[SXY, q, at, :] += once * exy


def planes(low, high, body):
    def step(q, carry):
        body(q)
        return carry

    lax.fori_loop(low, high, step, 0)


def clear_edges(w, slots):
    zero = jnp.zeros((PAD, 128), jnp.float32)
    for field, top in ((VX, 1), (VY, 0), (VZ, 1), (SXY, 0), (SYY, 1), (SYZ, 0)):
        for slot in range(slots):
            w[field, slot, pl.ds(PAD + 64 if top else 0, PAD), :] = zero


def pack_kernel(with_mats, meta, state, lam, mu, buoy, *rest):
    if with_mats:
        cross, chip, w, b, sems, out_sems, mat_sems = rest
        crosses = (cross, cross)
    else:
        cross_0, cross_1, chip, w, b, sems, out_sems, mat_sems = rest
        crosses = (cross_0, cross_1)
    odd = lax.rem(meta[0], 2) == 1
    loads = []
    for side, first in ((0, 0), (1, 5)):
        loads.append(
            pltpu.make_async_copy(
                buoy.at[pl.ds(first, 3)], b.at[pl.ds(3 * side, 3)], sems.at[4 + side]
            )
        )
        for shot in range(2):
            loads.append(
                pltpu.make_async_copy(
                    state.at[:, shot, pl.ds(first, 3)],
                    w.at[shot, :, pl.ds(3 * side, 3), pl.ds(PAD, 64)],
                    sems.at[2 * shot + side],
                )
            )
    for load in loads:
        load.start()
    mats = []
    if with_mats:
        for rightward in (True, False):
            first = MATS_RIGHTWARD[0] if rightward else MATS_LEFTWARD[0]
            for i, array in enumerate((buoy, lam, mu)):
                mats.append((rightward, array.at[pl.ds(first, 2)], 2 * SENT + 2 * i))

    def send(rightward, to_cross):
        for i, (go_right, source, at) in enumerate(mats):
            if go_right == rightward:
                target = cross if to_cross else chip
                pltpu.make_async_copy(source, target.at[pl.ds(at, 2)], mat_sems.at[i]).start()

    @pl.when(odd)
    def _():
        send(True, True)
        send(False, False)

    @pl.when(jnp.logical_not(odd))
    def _():
        send(True, False)
        send(False, True)

    for shot in range(2):
        clear_edges(w.at[shot], 6)
    for load in loads:
        load.wait()
    factor = courant if with_mats else -courant
    kb = lambda q, flat: factor * b[q, flat, :]
    for shot in range(2):
        velocity = functools.partial(velocity_plane, w.at[shot], kb)
        planes(1, 3, velocity)
        planes(4, 6, velocity)

    def copies(shot, rightward, to_cross):
        base = 0
        result = []
        for i, (field, first, count, _) in enumerate(RIGHTWARD if rightward else LEFTWARD):
            slot = first if first < 3 else first - 2
            if to_cross:
                target = crosses[shot].at[pl.ds((SENT * shot if with_mats else 0) + base, count)]
            else:
                target = chip.at[pl.ds(SENT * shot + base, count)]
            result.append(
                pltpu.make_async_copy(
                    w.at[shot, field, pl.ds(slot, count), pl.ds(PAD, 64)],
                    target,
                    out_sems.at[shot, 0 if rightward else 1, i],
                )
            )
            base += count
        return result

    def run(action):
        @pl.when(odd)
        def _():
            for shot in range(2):
                for copy in copies(shot, True, True) + copies(shot, False, False):
                    action(copy)

        @pl.when(jnp.logical_not(odd))
        def _():
            for shot in range(2):
                for copy in copies(shot, True, False) + copies(shot, False, True):
                    action(copy)

    run(lambda copy: copy.start())
    run(lambda copy: copy.wait())
    for i, (_, source, at) in enumerate(mats):
        pltpu.make_async_copy(source, cross.at[pl.ds(at, 2)], mat_sems.at[i]).wait()


def pack(meta, state, lam, mu, buoy, with_mats):
    anywhere = pl.BlockSpec(memory_space=pl.ANY)
    big = jax.ShapeDtypeStruct((2 * SENT + (6 if with_mats else 0), 64, 128), jnp.float32)
    half = jax.ShapeDtypeStruct((SENT, 64, 128), jnp.float32)
    out = (big, big) if with_mats else (half, half, big)
    return pl.pallas_call(
        functools.partial(pack_kernel, with_mats),
        out_shape=out,
        in_specs=[pl.BlockSpec(memory_space=pltpu.SMEM)] + [anywhere] * 4,
        out_specs=tuple(anywhere for _ in out),
        scratch_shapes=[
            pltpu.VMEM((2, 9, 6, 64 + 2 * PAD, 128), jnp.float32),
            pltpu.VMEM((6, 64, 128), jnp.float32),
            pltpu.SemaphoreType.DMA((6,)),
            pltpu.SemaphoreType.DMA((2, 2, 9)),
            pltpu.SemaphoreType.DMA((6,)),
        ],
        compiler_params=pltpu.CompilerParams(vmem_limit_bytes=12 << 20),
        name="pack_forward" if with_mats else "pack_adjoint",
    )(meta, state, lam, mu, buoy)


def load_mats(meta, lam, mu, buoy, cross, chip, mats, sems, action):
    odd = lax.rem(meta[0], 2) == 1
    for i, array in enumerate((buoy, lam, mu)):
        action(pltpu.make_async_copy(array, mats.at[i, pl.ds(OWN, 8)], sems.at[i, 0]))

    def halo(left, right):
        for i in range(3):
            at = pl.ds(2 * SENT + 2 * i, 2)
            action(pltpu.make_async_copy(left.at[at], mats.at[i, pl.ds(1, 2)], sems.at[i, 1]))
            action(pltpu.make_async_copy(right.at[at], mats.at[i, pl.ds(11, 2)], sems.at[i, 2]))

    @pl.when(odd)
    def _():
        halo(chip, cross)

    @pl.when(jnp.logical_not(odd))
    def _():
        halo(cross, chip)


def load_state(meta, state, shot, cross, cross_base, chip, w, sems, action):
    odd = lax.rem(meta[0], 2) == 1
    action(
        pltpu.make_async_copy(
            state.at[:, shot], w.at[:, pl.ds(OWN, 8), pl.ds(PAD, 64)], sems.at[0, 0]
        )
    )

    def halo(left, left_base, right, right_base):
        for side, ref, base, table in (
            (1, left, left_base, RIGHTWARD),
            (2, right, right_base, LEFTWARD),
        ):
            for i, (field, _, count, slot) in enumerate(table):
                action(
                    pltpu.make_async_copy(
                        ref.at[pl.ds(base, count)],
                        w.at[field, pl.ds(slot, count), pl.ds(PAD, 64)],
                        sems.at[side, i],
                    )
                )
                base += count

    @pl.when(odd)
    def _():
        halo(chip, SENT * shot, cross, cross_base)

    @pl.when(jnp.logical_not(odd))
    def _():
        halo(cross, cross_base, chip, SENT * shot)


def scale_mats(mats, factor):
    def one(q):
        mats[0, q] = factor * mats[0, q]
        mats[1, q] = factor * mats[1, q]
        mats[2, q] = (2.0 * factor) * mats[2, q]

    planes(1, 13, one)


def start(copy):
    copy.start()


def wait(copy):
    copy.wait()


def forward_kernel(
    meta, src_index, src_amp, state, lam, mu, buoy, cross, chip, strains, w, mats, mat_sems, sems
):
    load_mats(meta, lam, mu, buoy, cross, chip, mats, mat_sems, start)
    for shot in range(2):
        load_state(meta, state, shot, cross, SENT * shot, chip, w.at[shot], sems.at[shot], start)
    for shot in range(2):
        clear_edges(w.at[shot], SLOTS)
    load_mats(meta, lam, mu, buoy, cross, chip, mats, mat_sems, wait)
    scale_mats(mats, courant)
    kb = lambda q, flat: mats[0, q, flat, :]
    for shot in range(2):
        u = w.at[shot]
        load_state(meta, state, shot, cross, SENT * shot, chip, u, sems.at[shot], wait)

        def strain_only(moment, q):
            for begin in range(0, 64, CHUNK):
                for i, value in enumerate(strain_chunk(u, q, begin)):
                    strains[shot, moment, i, q - OWN, pl.ds(begin, CHUNK), :] = value

        def own(moment, q):
            for begin in range(0, 64, CHUNK):
                strain = strain_chunk(u, q, begin)
                for i, value in enumerate(strain):
                    strains[shot, moment, i, q - OWN, pl.ds(begin, CHUNK), :] = value
                stress_chunk(u, mats, q, begin, strain)

        def outer(q):
            for begin in range(0, 64, CHUNK):
                stress_chunk(u, mats, q, begin, strain_chunk(u, q, begin))

        cell = src_index[shot]
        slot = lax.shift_right_logical(cell, 13) - 8 * meta[0] + OWN
        row = jnp.bitwise_and(lax.shift_right_logical(cell, 7), 63) + PAD
        lane = jnp.bitwise_and(cell, 127)

        def source(moment, low, high):
            @pl.when(jnp.logical_and(slot >= low, slot < high))
            def _():
                amount = jnp.where(lanes(1) == lane, src_amp[shot, moment], 0.0)
                for field in (SXX, SYY, SZZ):
                    u[field, slot, pl.ds(row, 1), :] += amount

        velocity = functools.partial(velocity_plane, u, kb)
        planes(OWN, OWN + 9, velocity)
        planes(1, 3, outer)
        planes(OWN, OWN + 8, functools.partial(own, 0))
        planes(11, 13, outer)
        source(0, 1, 13)
        planes(OWN - 1, OWN + 10, velocity)
        planes(2, 3, outer)
        planes(OWN, OWN + 8, functools.partial(own, 1))
        planes(11, 12, outer)
        source(1, 2, 12)
        planes(OWN, OWN + 9, velocity)
        planes(OWN, OWN + 8, functools.partial(strain_only, 2))


def forward(meta, src_index, src_amp, state, lam, mu, buoy, cross, chip):
    anywhere = pl.BlockSpec(memory_space=pl.ANY)
    scalars = pl.BlockSpec(memory_space=pltpu.SMEM)
    return pl.pallas_call(
        forward_kernel,
        out_shape=jax.ShapeDtypeStruct((2, 3, 6, 8, 64, 128), jnp.float32),
        in_specs=[scalars] * 3 + [anywhere] * 6,
        out_specs=pl.BlockSpec(memory_space=pltpu.VMEM),
        scratch_shapes=[
            pltpu.VMEM((2, 9, SLOTS, 64 + 2 * PAD, 128), jnp.float32),
            pltpu.VMEM((3, SLOTS, 64, 128), jnp.float32),
            pltpu.SemaphoreType.DMA((3, 3)),
            pltpu.SemaphoreType.DMA((2, 3, 9)),
        ],
        compiler_params=pltpu.CompilerParams(vmem_limit_bytes=24 << 20),
        name="forward_steps",
    )(meta, src_index, src_amp, state, lam, mu, buoy, cross, chip)


def inject_kernel(meta, cells, amounts, out, rows_hot, values):
    base = (8 * meta[0] - OWN) * 64
    for shot in range(2):
        cell = cells[pl.ds(shot, 1), :]
        count = cell.shape[1]
        row = lax.shift_right_logical(cell, 7) - base
        lane = jnp.bitwise_and(cell, 127)

        def hot(k, carry):
            at = k * 128 + lax.broadcasted_iota(jnp.int32, (128, count), 0)
            rows_hot[pl.ds(k * 128, 128), :] = jnp.where(at == row, 1.0, 0.0).astype(jnp.bfloat16)
            return carry

        lax.fori_loop(0, SLOTS * 64 // 128, hot, 0)
        lane_hot = lax.broadcasted_iota(jnp.int32, (128, count), 0) == lane
        for moment in range(3):
            left = amounts[shot, pl.ds(moment, 1), :]
            for part in range(3):
                piece = left.astype(jnp.bfloat16).astype(jnp.float32)
                left = left - piece
                values[part, pl.ds(128 * moment, 128), :] = jnp.where(lane_hot, piece, 0.0).astype(
                    jnp.bfloat16
                )
        dims = (((1,), (1,)), ((), ()))
        size = SLOTS * 64 // 2
        for k in range(2):
            hot_rows = rows_hot[pl.ds(k * size, size), :]
            total = None
            for part in range(3):
                product = lax.dot_general(
                    hot_rows, values[part], dims, preferred_element_type=jnp.float32
                )
                total = product if total is None else total + product
            for moment in range(3):
                out[shot, moment, pl.ds(k * size, size), :] = total[:, 128 * moment : 128 * moment + 128]


def inject(meta, cells, amounts):
    count = cells.shape[1]
    vmem = pl.BlockSpec(memory_space=pltpu.VMEM)
    return pl.pallas_call(
        inject_kernel,
        out_shape=jax.ShapeDtypeStruct((2, 3, SLOTS * 64, 128), jnp.float32),
        in_specs=[pl.BlockSpec(memory_space=pltpu.SMEM), vmem, vmem],
        out_specs=vmem,
        scratch_shapes=[
            pltpu.VMEM((SLOTS * 64, count), jnp.bfloat16),
            pltpu.VMEM((3, 384, count), jnp.bfloat16),
        ],
        compiler_params=pltpu.CompilerParams(vmem_limit_bytes=24 << 20),
        name="receivers",
    )(meta, cells, amounts)


def adjoint_kernel(
    shot, meta, state, lam, mu, buoy, f_cross, f_chip, cross, chip, strains, dense, *rest
):
    if shot == 0:
        grads, w, mats, mat_sems, sems = rest
    else:
        before, keep, give, grads, w, mats, mat_sems, sems = rest
    load_mats(meta, lam, mu, buoy, f_cross, f_chip, mats, mat_sems, start)
    load_state(meta, state, shot, cross, 0, chip, w, sems, start)
    clear_edges(w, SLOTS)
    load_mats(meta, lam, mu, buoy, f_cross, f_chip, mats, mat_sems, wait)
    scale_mats(mats, -courant)
    load_state(meta, state, shot, cross, 0, chip, w, sems, wait)
    kb = lambda q, flat: mats[0, q, flat, :]

    def own(moment, stress, q):
        p = q - OWN
        for begin in range(0, 64, CHUNK):
            flat = pl.ds(begin, CHUNK)
            exx, eyy, ezz, eyz, exz, exy = strain_chunk(w, q, begin)
            fxx, fyy, fzz, fyz, fxz, fxy = [strains[shot, moment, i, p, flat, :] for i in range(6)]
            bulk = (fxx + fyy + fzz) * (exx + eyy + ezz)
            shear = 2.0 * (fxx * exx + fyy * eyy + fzz * ezz) + (
                fyz * eyz + fxz * exz + fxy * exy
            )
            if moment < 2:
                bulk, shear = bulk + grads[0, p, flat, :], shear + grads[1, p, flat, :]
            elif shot == 1:
                bulk, shear = bulk + before[0, p, flat, :], shear + before[1, p, flat, :]
            grads[0, p, flat, :] = bulk
            grads[1, p, flat, :] = shear
            if stress:
                stress_chunk(w, mats, q, begin, (exx, eyy, ezz, eyz, exz, exy))

    def outer(q):
        for begin in range(0, 64, CHUNK):
            stress_chunk(w, mats, q, begin, strain_chunk(w, q, begin))

    def velocity(moment, q):
        velocity_plane(w, kb, q, dense.at[shot, moment])

    for slot in (1, 2, 12, 13):
        w[VZ, slot, pl.ds(PAD, 64), :] += dense[shot, 2, slot]
    planes(OWN, OWN + 9, functools.partial(velocity, 2))
    planes(1, 3, outer)
    planes(OWN, OWN + 8, functools.partial(own, 2, True))
    planes(11, 13, outer)
    planes(OWN - 1, OWN + 10, functools.partial(velocity, 1))
    planes(2, 3, outer)
    planes(OWN, OWN + 8, functools.partial(own, 1, True))
    planes(11, 12, outer)
    planes(OWN, OWN + 9, functools.partial(velocity, 0))
    planes(OWN, OWN + 8, functools.partial(own, 0, False))
    if shot == 1:
        mine = pl.multiple_of(meta[1] * 32, 32)
        keep[...] = grads[:, :, pl.ds(mine, 32), :]
        give[...] = grads[:, :, pl.ds(pl.multiple_of(32 - mine, 32), 32), :]


def adjoint(shot, meta, state, lam, mu, buoy, f_cross, f_chip, cross, chip, strains, dense, before):
    anywhere = pl.BlockSpec(memory_space=pl.ANY)
    vmem = pl.BlockSpec(memory_space=pltpu.VMEM)
    whole = jax.ShapeDtypeStruct((2, 8, 64, 128), jnp.float32)
    half = jax.ShapeDtypeStruct((2, 8, 32, 128), jnp.float32)
    scratch = [
        pltpu.VMEM((9, SLOTS, 64 + 2 * PAD, 128), jnp.float32),
        pltpu.VMEM((3, SLOTS, 64, 128), jnp.float32),
        pltpu.SemaphoreType.DMA((3, 3)),
        pltpu.SemaphoreType.DMA((3, 9)),
    ]
    operands = [meta, state, lam, mu, buoy, f_cross, f_chip, cross, chip, strains, dense]
    in_specs = [pl.BlockSpec(memory_space=pltpu.SMEM)] + [anywhere] * 8 + [vmem] * 2
    if shot == 0:
        out_shape, out_specs = whole, vmem
    else:
        operands.append(before)
        in_specs.append(vmem)
        out_shape, out_specs = (half, half), (vmem, vmem)
        scratch = [pltpu.VMEM(whole.shape, jnp.float32)] + scratch
    return pl.pallas_call(
        functools.partial(adjoint_kernel, shot),
        out_shape=out_shape,
        in_specs=in_specs,
        out_specs=out_specs,
        scratch_shapes=scratch,
        compiler_params=pltpu.CompilerParams(vmem_limit_bytes=28 << 20),
        name="adjoint_steps",
    )(*operands)


def shards(
    lame_lambda, lame_shear, buoyancy, fwd_state, adj_state, src_index, src_amp, recv_index, residual
):
    count = lax.axis_size("space")
    onchip = [(i, i + 1) for i in range(0, count, 2)] + [(i + 1, i) for i in range(0, count, 2)]
    between = [(i, i + 1) for i in range(1, count - 1, 2)]
    between = between + [(j, i) for i, j in between]
    swap_chips = lambda x: lax.ppermute(x, "space", between)
    swap_cores = lambda x: lax.ppermute(x, "space", onchip)
    meta = jnp.stack([lax.axis_index("space"), lax.axis_index("shot")]).astype(jnp.int32)
    mats = (lame_lambda, lame_shear, buoyancy)
    f_cross, f_chip = pack(meta, fwd_state, *mats, True)
    f_cross = swap_chips(f_cross)
    a_cross_0, a_cross_1, a_chip = pack(meta, adj_state, *mats, False)
    a_cross_0 = swap_chips(a_cross_0)
    a_cross_1 = swap_chips(a_cross_1)
    f_chip = swap_cores(f_chip)
    a_chip = swap_cores(a_chip)
    dense = inject(meta, recv_index, residual).reshape(2, 3, SLOTS, 64, 128)
    strains = forward(meta, src_index, src_amp, fwd_state, *mats, f_cross, f_chip)
    grads = adjoint(
        0, meta, adj_state, *mats, f_cross, f_chip, a_cross_0, a_chip, strains, dense, None
    )
    keep, give = adjoint(
        1, meta, adj_state, *mats, f_cross, f_chip, a_cross_1, a_chip, strains, dense, grads
    )
    total = keep + lax.ppermute(give, "shot", [(0, 1), (1, 0)])
    return (total[0], total[1])


def solution(mesh):
    in_specs = (
        P("space", None, None),
        P("space", None, None),
        P("space", None, None),
        P(None, "shot", "space", None, None),
        P(None, "shot", "space", None, None),
        P("shot"),
        P("shot", None),
        P("shot", None),
        P("shot", None, None),
    )
    out_specs = (P("space", "shot", None), P("space", "shot", None))
    return jax.shard_map(shards, mesh=mesh, in_specs=in_specs, out_specs=out_specs, check_vma=False)
```

```python
import functools

import jax
import jax.numpy as jnp
from jax import lax
from jax.experimental import pallas as pl
from jax.experimental.pallas import tpu as pltpu
from jax.sharding import PartitionSpec as P

courant = 0.2
VX, VY, VZ, SXX, SYY, SZZ, SYZ, SXZ, SXY = range(9)

SLOTS = 14
OWN = 3
PAD = 8

RIGHTWARD = (
    (VX, 5, 3, 0), (VY, 6, 2, 1), (VZ, 6, 2, 1), (SXX, 6, 2, 1), (SYY, 7, 1, 2), (SZZ, 7, 1, 2),
    (SYZ, 7, 1, 2), (SXZ, 6, 2, 1), (SXY, 6, 2, 1),
)
LEFTWARD = (
    (VX, 0, 2, 11), (VY, 0, 3, 11), (VZ, 0, 3, 11), (SXX, 0, 2, 11), (SYY, 0, 2, 11), (SZZ, 0, 2, 11),
    (SYZ, 0, 2, 11), (SXZ, 0, 2, 11), (SXY, 0, 2, 11),
)
MATS_RIGHTWARD = (6, 1)
MATS_LEFTWARD = (0, 11)
SENT = 20
CHUNK = 16


def of_shot(w, shot):
    return [ref.at[shot] for ref in w]


def lanes(rows):
    return lax.broadcasted_iota(jnp.int32, (rows, 128), 1)


def below_z(x):
    return jnp.where(lanes(x.shape[0]) == 0, 0.0, pltpu.roll(x, 1, 1))


def above_z(x):
    return jnp.where(lanes(x.shape[0]) == 127, 0.0, pltpu.roll(x, 127, 1))


def velocity_plane(w, kb, q, inject=None):
    for start in range(0, 64, CHUNK):
        at = pl.ds(PAD + start, CHUNK)
        down = pl.ds(PAD + start - 1, CHUNK)
        up = pl.ds(PAD + start + 1, CHUNK)
        flat = pl.ds(start, CHUNK)
        xy_b, xz_b = w[SXY][q - 1, at, :], w[SXZ][q - 1, at, :]
        new_x = w[VX][q - 1, at, :] + kb(q - 1, flat) * (
            (w[SXX][q, at, :] - w[SXX][q - 1, at, :])
            + (xy_b - w[SXY][q - 1, down, :])
            + (xz_b - below_z(xz_b))
        )
        yz, zz = w[SYZ][q, at, :], w[SZZ][q, at, :]
        scaled = kb(q, flat)
        new_y = w[VY][q, at, :] + scaled * (
            (w[SXY][q, at, :] - xy_b) + (w[SYY][q, up, :] - w[SYY][q, at, :]) + (yz - below_z(yz))
        )
        new_z = w[VZ][q, at, :] + scaled * (
            (w[SXZ][q, at, :] - xz_b) + (yz - w[SYZ][q, down, :]) + (above_z(zz) - zz)
        )
        if inject is not None:
            new_z = new_z + inject[q, flat, :]
        w[VX][q - 1, at, :] = new_x
        w[VY][q, at, :] = new_y
        w[VZ][q, at, :] = new_z


def strain_chunk(w, q, start):
    at = pl.ds(PAD + start, CHUNK)
    down = pl.ds(PAD + start - 1, CHUNK)
    up = pl.ds(PAD + start + 1, CHUNK)
    vx, vy, vz = w[VX][q, at, :], w[VY][q, at, :], w[VZ][q, at, :]
    exx = vx - w[VX][q - 1, at, :]
    eyy = vy - w[VY][q, down, :]
    ezz = vz - below_z(vz)
    eyz = (above_z(vy) - vy) + (w[VZ][q, up, :] - vz)
    exz = (above_z(vx) - vx) + (w[VZ][q + 1, at, :] - vz)
    exy = (w[VX][q, up, :] - vx) + (w[VY][q + 1, at, :] - vy)
    return exx, eyy, ezz, eyz, exz, exy


def stress_chunk(w, mats, q, start, strain, sign=1.0):
    at = pl.ds(PAD + start, CHUNK)
    flat = pl.ds(start, CHUNK)
    exx, eyy, ezz, eyz, exz, exy = strain
    twice = mats[2, q, flat, :]
    bulk = mats[1, q, flat, :] * (exx + eyy + ezz)
    once = 0.5 * twice
    for field, change in (
        (SXX, bulk + twice * exx),
        (SYY, bulk + twice * eyy),
        (SZZ, bulk + twice * ezz),
        (SYZ, once * eyz),
        (SXZ, once * exz),
        (SXY, once * exy),
    ):
        old = w[field][q, at, :]
        w[field][q, at, :] = old + change if sign > 0 else old - change


UNROLL = 4


def planes(low, high, body):
    whole = (high - low) // UNROLL

    def step(i, carry):
        for j in range(UNROLL):
            body(low + UNROLL * i + j)
        return carry

    lax.fori_loop(0, whole, step, 0)
    for q in range(low + whole * UNROLL, high):
        body(q)


def clear_edges(w, slots):
    zero = jnp.zeros((PAD, 128), jnp.float32)
    for field, top in ((VX, 1), (VY, 0), (VZ, 1), (SXY, 0), (SYY, 1), (SYZ, 0)):
        for slot in range(slots):
            w[field][slot, pl.ds(PAD + 64 if top else 0, PAD), :] = zero


def velocity_values(w, scaled, q):
    at, down, up = pl.ds(PAD, 64), pl.ds(PAD - 1, 64), pl.ds(PAD + 1, 64)
    xy_b, xz_b = w[SXY, q - 1, at, :], w[SXZ, q - 1, at, :]
    new_x = w[VX, q - 1, at, :] + scaled(q - 1) * (
        (w[SXX, q, at, :] - w[SXX, q - 1, at, :])
        + (xy_b - w[SXY, q - 1, down, :])
        + (xz_b - below_z(xz_b))
    )
    yz, zz = w[SYZ, q, at, :], w[SZZ, q, at, :]
    new_y = w[VY, q, at, :] + scaled(q) * (
        (w[SXY, q, at, :] - xy_b) + (w[SYY, q, up, :] - w[SYY, q, at, :]) + (yz - below_z(yz))
    )
    new_z = w[VZ, q, at, :] + scaled(q) * (
        (w[SXZ, q, at, :] - xz_b) + (yz - w[SYZ, q, down, :]) + (above_z(zz) - zz)
    )
    return new_x, new_y, new_z


def pack_kernel(with_mats, meta, state, lam, mu, buoy, *rest):
    if with_mats:
        cross, chip, w, b, sems, mat_sems = rest
        crosses = (cross.at[pl.ds(0, SENT)], cross.at[pl.ds(SENT, SENT)])
    else:
        cross_0, cross_1, chip, w, b, sems, mat_sems = rest
        crosses = (cross_0, cross_1)
    odd = lax.rem(meta[0], 2) == 1
    loads = {}
    for side, first in ((0, 0), (1, 5)):
        loads[2, side] = pltpu.make_async_copy(
            buoy.at[pl.ds(first, 3)], b.at[side], sems.at[2, side]
        )
    for shot in range(2):
        for side, first in ((0, 0), (1, 5)):
            loads[shot, side] = pltpu.make_async_copy(
                state.at[:, shot, pl.ds(first, 3)],
                w.at[shot, side, :, :, pl.ds(PAD, 64)],
                sems.at[shot, side],
            )
    for load in loads.values():
        load.start()
    mats = []
    if with_mats:
        for side, first in ((1, MATS_RIGHTWARD[0]), (0, MATS_LEFTWARD[0])):
            for i, array in enumerate((buoy, lam, mu)):
                mats.append((side, array.at[pl.ds(first, 2)], 2 * SENT + 2 * i))
    zero = jnp.zeros((PAD, 128), jnp.float32)
    for shot in range(2):
        for side in range(2):
            for field, row in ((SXY, 0), (SYZ, 0), (SYY, PAD + 64)):
                for slot in range(3):
                    w[shot, side, field, slot, pl.ds(row, PAD), :] = zero
    factor = courant if with_mats else -courant

    def send(to_cross):
        for i, (side, source, at) in enumerate(mats):
            target = cross if side == to_cross else chip
            pltpu.make_async_copy(source, target.at[pl.ds(at, 2)], mat_sems.at[i]).start()
        loads[2, 0].wait()
        loads[2, 1].wait()
        for shot in range(2):
            for side, table in ((1, RIGHTWARD), (0, LEFTWARD)):
                loads[shot, side].wait()
                slab = w.at[shot, side]
                out = crosses[shot] if side == to_cross else chip.at[pl.ds(SENT * shot, SENT)]
                fresh = {}
                for q in (1, 2):
                    values = velocity_values(slab, lambda i: factor * b[side, i], q)
                    fresh[VX, q - 1], fresh[VY, q], fresh[VZ, q] = values
                base = 0
                for field, first, count, _ in table:
                    for i in range(count):
                        slot = first + i - 5 * side
                        value = fresh.get((field, slot))
                        if value is None:
                            value = slab[field, slot, pl.ds(PAD, 64), :]
                        out[base + i] = value
                    base += count
        for i, (side, source, at) in enumerate(mats):
            target = cross if side == to_cross else chip
            pltpu.make_async_copy(source, target.at[pl.ds(at, 2)], mat_sems.at[i]).wait()

    @pl.when(odd)
    def _():
        send(1)

    @pl.when(jnp.logical_not(odd))
    def _():
        send(0)


def pack(meta, state, lam, mu, buoy, with_mats):
    hbm = pl.BlockSpec(memory_space=pltpu.HBM)
    big = jax.ShapeDtypeStruct((2 * SENT + (6 if with_mats else 0), 64, 128), jnp.float32)
    half = jax.ShapeDtypeStruct((SENT, 64, 128), jnp.float32)
    out = (big, big) if with_mats else (half, half, big)
    return pl.pallas_call(
        functools.partial(pack_kernel, with_mats),
        out_shape=out,
        in_specs=[pl.BlockSpec(memory_space=pltpu.SMEM)] + [hbm] * 4,
        out_specs=tuple(pl.BlockSpec(memory_space=pltpu.VMEM) for _ in out),
        scratch_shapes=[
            pltpu.VMEM((2, 2, 9, 3, 64 + 2 * PAD, 128), jnp.float32),
            pltpu.VMEM((2, 3, 64, 128), jnp.float32),
            pltpu.SemaphoreType.DMA((3, 2)),
            pltpu.SemaphoreType.DMA((6,)),
        ],
        compiler_params=pltpu.CompilerParams(vmem_limit_bytes=16 << 20),
        name="pack_forward" if with_mats else "pack_adjoint",
    )(meta, state, lam, mu, buoy)


def by_side(meta, cross, chip, action):
    odd = lax.rem(meta[0], 2) == 1

    @pl.when(odd)
    def _():
        action(chip, cross)

    @pl.when(jnp.logical_not(odd))
    def _():
        action(cross, chip)


def load_mats(meta, lam, mu, buoy, cross, chip, mats):
    scales = (courant, courant, 2.0 * courant)

    def own(p):
        for i, array in enumerate((buoy, lam, mu)):
            mats[i, p + OWN] = scales[i] * array[p]

    planes(0, 8, own)

    def halo(left, right):
        for i in range(3):
            for j in range(2):
                mats[i, 1 + j] = scales[i] * left[2 * SENT + 2 * i + j]
                mats[i, 11 + j] = scales[i] * right[2 * SENT + 2 * i + j]

    by_side(meta, cross, chip, halo)


def load_state(meta, state, shot, cross, chip, w):
    def own(p):
        for field in range(9):
            w[field][p + OWN, pl.ds(PAD, 64), :] = state[field, shot, p]

    planes(0, 8, own)

    def halo(left, right):
        for ref, table in ((left, RIGHTWARD), (right, LEFTWARD)):
            base = 0
            for field, _, count, slot in table:
                for i in range(count):
                    w[field][slot + i, pl.ds(PAD, 64), :] = ref[base + i]
                base += count

    by_side(meta, cross, chip, halo)


def forward_kernel(
    meta, src_index, src_amp, state, lam, mu, buoy, cross, chip, strains, mats, *w_both
):
    for shot in range(2):
        clear_edges(of_shot(w_both, shot), SLOTS)
    load_mats(meta, lam, mu, buoy, cross, chip, mats)
    kb = lambda q, flat: mats[0, q, flat, :]
    for shot in range(2):
        u = of_shot(w_both, shot)
        part = pl.ds(SENT * shot, SENT)
        load_state(meta, state, shot, cross.at[part], chip.at[part], u)

        def strain_only(moment, q):
            for begin in range(0, 64, CHUNK):
                for i, value in enumerate(strain_chunk(u, q, begin)):
                    strains[shot, moment, i, q - OWN, pl.ds(begin, CHUNK), :] = value

        def own(moment, q):
            for begin in range(0, 64, CHUNK):
                strain = strain_chunk(u, q, begin)
                for i, value in enumerate(strain):
                    strains[shot, moment, i, q - OWN, pl.ds(begin, CHUNK), :] = value
                stress_chunk(u, mats, q, begin, strain)

        def outer(q):
            for begin in range(0, 64, CHUNK):
                stress_chunk(u, mats, q, begin, strain_chunk(u, q, begin))

        cell = src_index[shot]
        slot = lax.shift_right_logical(cell, 13) - 8 * meta[0] + OWN
        row = jnp.bitwise_and(lax.shift_right_logical(cell, 7), 63) + PAD
        lane = jnp.bitwise_and(cell, 127)

        def source(moment, low, high):
            @pl.when(jnp.logical_and(slot >= low, slot < high))
            def _():
                amount = jnp.where(lanes(1) == lane, src_amp[shot, moment], 0.0)
                for field in (SXX, SYY, SZZ):
                    u[field][slot, pl.ds(row, 1), :] += amount

        velocity = functools.partial(velocity_plane, u, kb)
        planes(OWN, OWN + 9, velocity)
        planes(1, 3, outer)
        planes(OWN, OWN + 8, functools.partial(own, 0))
        planes(11, 13, outer)
        source(0, 1, 13)
        planes(OWN - 1, OWN + 10, velocity)
        planes(2, 3, outer)
        planes(OWN, OWN + 8, functools.partial(own, 1))
        planes(11, 12, outer)
        source(1, 2, 12)
        planes(OWN, OWN + 9, velocity)
        planes(OWN, OWN + 8, functools.partial(strain_only, 2))


def forward(meta, src_index, src_amp, state, lam, mu, buoy, cross, chip):
    vmem = pl.BlockSpec(memory_space=pltpu.VMEM)
    scalars = pl.BlockSpec(memory_space=pltpu.SMEM)
    return pl.pallas_call(
        forward_kernel,
        out_shape=(
            jax.ShapeDtypeStruct((2, 3, 6, 8, 64, 128), jnp.float32),
            jax.ShapeDtypeStruct((3, SLOTS, 64, 128), jnp.float32),
        ),
        in_specs=[scalars] * 3 + [vmem] * 6,
        out_specs=(vmem, vmem),
        scratch_shapes=[pltpu.VMEM((2, SLOTS, 64 + 2 * PAD, 128), jnp.float32)] * 9,
        compiler_params=pltpu.CompilerParams(vmem_limit_bytes=28 << 20),
        name="forward_steps",
    )(meta, src_index, src_amp, state, lam, mu, buoy, cross, chip)


def inject_kernel(meta, cells, amounts, out, rows_hot, values):
    base = (8 * meta[0] - OWN) * 64
    for shot in range(2):
        cell = cells[pl.ds(shot, 1), :]
        count = cell.shape[1]
        row = lax.shift_right_logical(cell, 7) - base
        lane = jnp.bitwise_and(cell, 127)

        def hot(k, carry):
            at = k * 128 + lax.broadcasted_iota(jnp.int32, (128, count), 0)
            rows_hot[pl.ds(k * 128, 128), :] = jnp.where(at == row, 1.0, 0.0).astype(jnp.bfloat16)
            return carry

        lax.fori_loop(0, SLOTS * 64 // 128, hot, 0)
        lane_hot = lax.broadcasted_iota(jnp.int32, (128, count), 0) == lane
        for moment in range(3):
            left = amounts[shot, pl.ds(moment, 1), :]
            for part in range(3):
                piece = left.astype(jnp.bfloat16).astype(jnp.float32)
                left = left - piece
                values[part, pl.ds(128 * moment, 128), :] = jnp.where(lane_hot, piece, 0.0).astype(
                    jnp.bfloat16
                )
        dims = (((1,), (1,)), ((), ()))
        size = SLOTS * 64 // 2
        for k in range(2):
            hot_rows = rows_hot[pl.ds(k * size, size), :]
            total = None
            for part in range(3):
                product = lax.dot_general(
                    hot_rows, values[part], dims, preferred_element_type=jnp.float32
                )
                total = product if total is None else total + product
            for moment in range(3):
                out[shot, moment, pl.ds(k * size, size), :] = total[:, 128 * moment : 128 * moment + 128]


def inject(meta, cells, amounts):
    count = cells.shape[1]
    vmem = pl.BlockSpec(memory_space=pltpu.VMEM)
    return pl.pallas_call(
        inject_kernel,
        out_shape=jax.ShapeDtypeStruct((2, 3, SLOTS * 64, 128), jnp.float32),
        in_specs=[pl.BlockSpec(memory_space=pltpu.SMEM), vmem, vmem],
        out_specs=vmem,
        scratch_shapes=[
            pltpu.VMEM((SLOTS * 64, count), jnp.bfloat16),
            pltpu.VMEM((3, 384, count), jnp.bfloat16),
        ],
        compiler_params=pltpu.CompilerParams(vmem_limit_bytes=24 << 20),
        name="receivers",
    )(meta, cells, amounts)


def adjoint_kernel(shot, meta, state, mats, cross, chip, strains, dense, *rest):
    if shot == 0:
        grads, *w = rest
    else:
        before, keep, give, grads, *w = rest
    clear_edges(w, SLOTS)
    load_state(meta, state, shot, cross, chip.at[pl.ds(SENT * shot, SENT)], w)
    kb = lambda q, flat: -mats[0, q, flat, :]

    def own(moment, stress, q):
        p = q - OWN
        for begin in range(0, 64, CHUNK):
            flat = pl.ds(begin, CHUNK)
            exx, eyy, ezz, eyz, exz, exy = strain_chunk(w, q, begin)
            fxx, fyy, fzz, fyz, fxz, fxy = [strains[shot, moment, i, p, flat, :] for i in range(6)]
            bulk = (fxx + fyy + fzz) * (exx + eyy + ezz)
            shear = 2.0 * (fxx * exx + fyy * eyy + fzz * ezz) + (
                fyz * eyz + fxz * exz + fxy * exy
            )
            if moment < 2:
                bulk, shear = bulk + grads[0, p, flat, :], shear + grads[1, p, flat, :]
            elif shot == 1:
                bulk, shear = bulk + before[0, p, flat, :], shear + before[1, p, flat, :]
            grads[0, p, flat, :] = bulk
            grads[1, p, flat, :] = shear
            if stress:
                stress_chunk(w, mats, q, begin, (exx, eyy, ezz, eyz, exz, exy), -1.0)

    def outer(q):
        for begin in range(0, 64, CHUNK):
            stress_chunk(w, mats, q, begin, strain_chunk(w, q, begin), -1.0)

    def velocity(moment, q):
        velocity_plane(w, kb, q, dense.at[shot, moment])

    for slot in (1, 2, 12, 13):
        w[VZ][slot, pl.ds(PAD, 64), :] += dense[shot, 2, slot]
    planes(OWN, OWN + 9, functools.partial(velocity, 2))
    planes(1, 3, outer)
    planes(OWN, OWN + 8, functools.partial(own, 2, True))
    planes(11, 13, outer)
    planes(OWN - 1, OWN + 10, functools.partial(velocity, 1))
    planes(2, 3, outer)
    planes(OWN, OWN + 8, functools.partial(own, 1, True))
    planes(11, 12, outer)
    planes(OWN, OWN + 9, functools.partial(velocity, 0))
    planes(OWN, OWN + 8, functools.partial(own, 0, False))
    if shot == 1:
        mine = pl.multiple_of(meta[1] * 32, 32)
        keep[...] = grads[:, :, pl.ds(mine, 32), :]
        give[...] = grads[:, :, pl.ds(pl.multiple_of(32 - mine, 32), 32), :]


def adjoint(shot, meta, state, mats, cross, chip, strains, dense, before):
    vmem = pl.BlockSpec(memory_space=pltpu.VMEM)
    whole = jax.ShapeDtypeStruct((2, 8, 64, 128), jnp.float32)
    half = jax.ShapeDtypeStruct((2, 8, 32, 128), jnp.float32)
    scratch = [pltpu.VMEM((SLOTS, 64 + 2 * PAD, 128), jnp.float32)] * 9
    operands = [meta, state, mats, cross, chip, strains, dense]
    out_shape, out_specs = whole, vmem
    if shot == 1:
        operands.append(before)
        out_shape, out_specs = (half, half), (vmem, vmem)
        scratch = [pltpu.VMEM(whole.shape, jnp.float32)] + scratch
    return pl.pallas_call(
        functools.partial(adjoint_kernel, shot),
        out_shape=out_shape,
        in_specs=[pl.BlockSpec(memory_space=pltpu.SMEM)] + [vmem] * (len(operands) - 1),
        out_specs=out_specs,
        scratch_shapes=scratch,
        compiler_params=pltpu.CompilerParams(vmem_limit_bytes=16 << 20),
        name="adjoint_steps",
    )(*operands)


def shards(
    lame_lambda, lame_shear, buoyancy, fwd_state, adj_state, src_index, src_amp, recv_index, residual
):
    count = lax.axis_size("space")
    onchip = [(i, i + 1) for i in range(0, count, 2)] + [(i + 1, i) for i in range(0, count, 2)]
    between = [(i, i + 1) for i in range(1, count - 1, 2)]
    between = between + [(j, i) for i, j in between]
    swap_chips = lambda x: lax.ppermute(x, "space", between)
    swap_cores = lambda x: lax.ppermute(x, "space", onchip)
    meta = jnp.stack([lax.axis_index("space"), lax.axis_index("shot")]).astype(jnp.int32)
    mats = (lame_lambda, lame_shear, buoyancy)
    f_cross, f_chip = pack(meta, fwd_state, *mats, True)
    f_cross = swap_chips(f_cross)
    a_cross_0, a_cross_1, a_chip = pack(meta, adj_state, *mats, False)
    a_cross_0 = swap_chips(a_cross_0)
    a_cross_1 = swap_chips(a_cross_1)
    f_chip = swap_cores(f_chip)
    a_chip = swap_cores(a_chip)
    dense = inject(meta, recv_index, residual).reshape(2, 3, SLOTS, 64, 128)
    strains, scaled = forward(meta, src_index, src_amp, fwd_state, *mats, f_cross, f_chip)
    grads = adjoint(
        0, meta, adj_state, scaled, a_cross_0, a_chip, strains, dense, None
    )
    keep, give = adjoint(
        1, meta, adj_state, scaled, a_cross_1, a_chip, strains, dense, grads
    )
    total = keep + lax.ppermute(give, "shot", [(0, 1), (1, 0)])
    return (total[0], total[1])


def solution(mesh):
    in_specs = (
        P("space", None, None),
        P("space", None, None),
        P("space", None, None),
        P(None, "shot", "space", None, None),
        P(None, "shot", "space", None, None),
        P("shot"),
        P("shot", None),
        P("shot", None),
        P("shot", None, None),
    )
    out_specs = (P("space", "shot", None), P("space", "shot", None))
    return jax.shard_map(shards, mesh=mesh, in_specs=in_specs, out_specs=out_specs, check_vma=False)
```

```python
import functools

import jax
import jax.numpy as jnp
from jax import lax
from jax.experimental import pallas as pl
from jax.experimental.pallas import tpu as pltpu
from jax.sharding import PartitionSpec as P

courant = 0.2
VX, VY, VZ, SXX, SYY, SZZ, SYZ, SXZ, SXY = range(9)

SLOTS = 14
OWN = 3
PAD = 8

NORMAL_X = (SXX, SXZ, SXY)
STRESSES = (SXX, SYY, SZZ, SYZ, SXZ, SXY)
RIGHTWARD = (
    ((VX, 1, "second"), (VX, 2, "raw"), (VY, 2, "second"), (VZ, 2, "second"))
    + tuple((field, 1, "fresh") for field in NORMAL_X)
    + tuple((field, 2, "raw") for field in STRESSES)
)
LEFTWARD = (
    ((VX, 11, "first"), (VY, 11, "raw"), (VY, 12, "first"), (VZ, 11, "raw"), (VZ, 12, "first"))
    + tuple((field, 11, "raw") for field in STRESSES)
    + tuple((field, 12, "fresh") for field in STRESSES)
)
MATS_RIGHTWARD = ((0, 6, 1), (0, 7, 2), (1, 7, 2), (2, 7, 2))
MATS_LEFTWARD = ((0, 0, 11), (0, 1, 12), (1, 0, 11), (2, 0, 11))
SENT = 17
SCALES = (courant, courant, 2.0 * courant)
VMEM_SPEC = pl.BlockSpec(memory_space=pltpu.VMEM)
SMEM_SPEC = pl.BlockSpec(memory_space=pltpu.SMEM)
SLABS = (jax.ShapeDtypeStruct((2, SLOTS, 64 + 2 * PAD, 128), jnp.float32),) * 9
STRAINS = jax.ShapeDtypeStruct((2, 3, 6, 8, 64, 128), jnp.float32)
MATS = jax.ShapeDtypeStruct((3, SLOTS, 64, 128), jnp.float32)
GRADS = jax.ShapeDtypeStruct((2, 8, 64, 128), jnp.float32)
CHUNK = 16


def of_shot(w, shot):
    return [ref.at[shot] for ref in w]


def lanes(rows):
    return lax.broadcasted_iota(jnp.int32, (rows, 128), 1)


def below_z(x):
    return jnp.where(lanes(x.shape[0]) == 0, 0.0, pltpu.roll(x, 1, 1))


def above_z(x):
    return jnp.where(lanes(x.shape[0]) == 127, 0.0, pltpu.roll(x, 127, 1))


def velocity_plane(w, kb, q, inject=None):
    for start in range(0, 64, CHUNK):
        at = pl.ds(PAD + start, CHUNK)
        down = pl.ds(PAD + start - 1, CHUNK)
        up = pl.ds(PAD + start + 1, CHUNK)
        flat = pl.ds(start, CHUNK)
        xy_b, xz_b = w[SXY][q - 1, at, :], w[SXZ][q - 1, at, :]
        new_x = w[VX][q - 1, at, :] + kb(q - 1, flat) * (
            (w[SXX][q, at, :] - w[SXX][q - 1, at, :])
            + (xy_b - w[SXY][q - 1, down, :])
            + (xz_b - below_z(xz_b))
        )
        yz, zz = w[SYZ][q, at, :], w[SZZ][q, at, :]
        scaled = kb(q, flat)
        new_y = w[VY][q, at, :] + scaled * (
            (w[SXY][q, at, :] - xy_b) + (w[SYY][q, up, :] - w[SYY][q, at, :]) + (yz - below_z(yz))
        )
        new_z = w[VZ][q, at, :] + scaled * (
            (w[SXZ][q, at, :] - xz_b) + (yz - w[SYZ][q, down, :]) + (above_z(zz) - zz)
        )
        if inject is not None:
            new_z = new_z + inject[q, flat, :]
        w[VX][q - 1, at, :] = new_x
        w[VY][q, at, :] = new_y
        w[VZ][q, at, :] = new_z


def strain_chunk(w, q, start):
    at = pl.ds(PAD + start, CHUNK)
    down = pl.ds(PAD + start - 1, CHUNK)
    up = pl.ds(PAD + start + 1, CHUNK)
    vx, vy, vz = w[VX][q, at, :], w[VY][q, at, :], w[VZ][q, at, :]
    exx = vx - w[VX][q - 1, at, :]
    eyy = vy - w[VY][q, down, :]
    ezz = vz - below_z(vz)
    eyz = (above_z(vy) - vy) + (w[VZ][q, up, :] - vz)
    exz = (above_z(vx) - vx) + (w[VZ][q + 1, at, :] - vz)
    exy = (w[VX][q, up, :] - vx) + (w[VY][q + 1, at, :] - vy)
    return exx, eyy, ezz, eyz, exz, exy


def stress_chunk(w, mats, q, start, strain, sign=1.0):
    at = pl.ds(PAD + start, CHUNK)
    flat = pl.ds(start, CHUNK)
    exx, eyy, ezz, eyz, exz, exy = strain
    twice = mats[2, q, flat, :]
    bulk = mats[1, q, flat, :] * (exx + eyy + ezz)
    once = 0.5 * twice
    for field, change in (
        (SXX, bulk + twice * exx),
        (SYY, bulk + twice * eyy),
        (SZZ, bulk + twice * ezz),
        (SYZ, once * eyz),
        (SXZ, once * exz),
        (SXY, once * exy),
    ):
        old = w[field][q, at, :]
        w[field][q, at, :] = old + change if sign > 0 else old - change


UNROLL = 2


def planes(low, count, body):
    whole = count // UNROLL

    def step(i, carry):
        for j in range(UNROLL):
            body(low + UNROLL * i + j)
        return carry

    if whole > 1:
        lax.fori_loop(0, whole, step, 0)
    else:
        for j in range(whole * UNROLL):
            body(low + j)
    for j in range(whole * UNROLL, count):
        body(low + j)


def clear_edges(w, slots):
    zero = jnp.zeros((PAD, 128), jnp.float32)
    for field, top in ((VX, 1), (VY, 0), (VZ, 1), (SXY, 0), (SYY, 1), (SYZ, 0)):
        for slot in range(slots):
            w[field][slot, pl.ds(PAD + 64 if top else 0, PAD), :] = zero


def early_velocities(w, shot, scaled, q, begin):
    at = pl.ds(PAD + begin, CHUNK)
    down = pl.ds(PAD + begin - 1, CHUNK)
    up = pl.ds(PAD + begin + 1, CHUNK)
    xy_b, xz_b = w[SXY][shot, q - 1, at, :], w[SXZ][shot, q - 1, at, :]
    new_x = w[VX][shot, q - 1, at, :] + scaled(q - 1) * (
        (w[SXX][shot, q, at, :] - w[SXX][shot, q - 1, at, :])
        + (xy_b - w[SXY][shot, q - 1, down, :])
        + (xz_b - below_z(xz_b))
    )
    yz, zz = w[SYZ][shot, q, at, :], w[SZZ][shot, q, at, :]
    new_y = w[VY][shot, q, at, :] + scaled(q) * (
        (w[SXY][shot, q, at, :] - xy_b)
        + (w[SYY][shot, q, up, :] - w[SYY][shot, q, at, :])
        + (yz - below_z(yz))
    )
    new_z = w[VZ][shot, q, at, :] + scaled(q) * (
        (w[SXZ][shot, q, at, :] - xz_b) + (yz - w[SYZ][shot, q, down, :]) + (above_z(zz) - zz)
    )
    return new_x, new_y, new_z


def pack_kernel(is_forward, meta, state, lam, mu, buoy, *rest):
    if is_forward:
        cross, chip, *w, early, edge, sems, edge_sems = rest
    else:
        cells, amounts, cross, chip, *w, early, edge, sems, edge_sems, hot, values, dense = rest
    odd = lax.rem(meta[0], 2) == 1
    edges = []
    for i, array in enumerate((buoy, lam, mu)):
        for side, first in ((0, 0), (1, 5)):
            edges.append(
                pltpu.make_async_copy(
                    array.at[pl.ds(first, 3)], edge.at[i, side], edge_sems.at[i, side]
                )
            )
    loads = [
        [
            pltpu.make_async_copy(
                state.at[field, shot],
                w[field].at[shot, pl.ds(OWN, 8), pl.ds(PAD, 64)],
                sems.at[shot, field],
            )
            for field in range(9)
        ]
        for shot in range(2)
    ]
    for load in edges + loads[0] + loads[1]:
        load.start()
    for shot in range(2):
        clear_edges(of_shot(w, shot), SLOTS)
    zero = jnp.zeros((PAD, 128), jnp.float32)
    for shot in range(2):
        for side in range(2):
            for field, row in ((VX, PAD + 64), (VY, 0), (VZ, PAD + 64)):
                for slot in range(2):
                    early[shot, side, field, slot, pl.ds(row, PAD), :] = zero
    if not is_forward:
        base = (8 * meta[0] - OWN) * 64
        for shot in range(2):
            cell = cells[pl.ds(shot, 1), :]
            for i, plane in enumerate((1, 2, 6, 7)):
                hot[pl.ds(64 * i, 64), :] = rows_of(cell, base, (plane + OWN) * 64, 64)
            split_values(amounts, shot, cell, (2,), values)
            dense[shot] = gathered(hot[...], values[...], 1)
    for load in edges:
        load.wait()
    factor = courant if is_forward else -courant

    def send(to_cross):
        for shot in range(2):
            for load in loads[shot]:
                load.wait()
            for side, table in ((1, RIGHTWARD), (0, LEFTWARD)):
                target = cross if side == to_cross else chip
                plane = 6 if side == 1 else 1
                new = early.at[shot, side]
                for j in range(2):
                    q = OWN + plane + j
                    for begin in range(0, 64, CHUNK):
                        at, flat = pl.ds(PAD + begin, CHUNK), pl.ds(begin, CHUNK)
                        scaled = lambda q: factor * edge[0, side, q - OWN - 5 * side, flat, :]
                        new_x, new_y, new_z = early_velocities(w, shot, scaled, q, begin)
                        if not is_forward:
                            row = 64 * (2 * side + j) + begin
                            new_z = new_z + dense[shot, pl.ds(row, CHUNK), :]
                        new[VX, j, at, :] = new_x
                        new[VY, j, at, :] = new_y
                        new[VZ, j, at, :] = new_z
                for begin in range(0, 64, CHUNK):
                    at, flat = pl.ds(PAD + begin, CHUNK), pl.ds(begin, CHUNK)
                    down, up = pl.ds(PAD + begin - 1, CHUNK), pl.ds(PAD + begin + 1, CHUNK)
                    vx, vy, vz = new[VX, 1, at, :], new[VY, 0, at, :], new[VZ, 0, at, :]
                    exx = vx - new[VX, 0, at, :]
                    eyy = vy - new[VY, 0, down, :]
                    ezz = vz - below_z(vz)
                    eyz = (above_z(vy) - vy) + (new[VZ, 0, up, :] - vz)
                    exz = (above_z(vx) - vx) + (new[VZ, 1, at, :] - vz)
                    exy = (new[VX, 1, up, :] - vx) + (new[VY, 1, at, :] - vy)
                    once = factor * edge[2, side, plane - 5 * side, flat, :]
                    twice = 2.0 * once
                    bulk = (factor * edge[1, side, plane - 5 * side, flat, :]) * (exx + eyy + ezz)
                    change = {
                        SXX: bulk + twice * exx,
                        SYY: bulk + twice * eyy,
                        SZZ: bulk + twice * ezz,
                        SYZ: once * eyz,
                        SXZ: once * exz,
                        SXY: once * exy,
                    }
                    for i, (field, _, kind) in enumerate(table):
                        if kind == "raw":
                            value = w[field][shot, OWN + 7 * side, at, :]
                        elif kind == "fresh":
                            value = w[field][shot, OWN + plane, at, :] + change[field]
                        else:
                            value = new[field, 0 if kind == "first" else 1, at, :]
                        target[SENT * shot + i, flat, :] = value
        if is_forward:
            for side, mats in ((1, MATS_RIGHTWARD), (0, MATS_LEFTWARD)):
                target = cross if side == to_cross else chip
                for i, (which, own, _) in enumerate(mats):
                    target[2 * SENT + i] = edge[which, side, own - 5 * side]

    @pl.when(odd)
    def _():
        send(1)

    @pl.when(jnp.logical_not(odd))
    def _():
        send(0)


def pack(meta, state, lam, mu, buoy, receivers):
    hbm = pl.BlockSpec(memory_space=pltpu.HBM)
    is_forward = receivers is None
    big = jax.ShapeDtypeStruct((2 * SENT + (4 if is_forward else 0), 64, 128), jnp.float32)
    out = (big, big) + SLABS
    whole = [pltpu.with_memory_space_constraint(x, pltpu.HBM) for x in (state, lam, mu, buoy)]
    extra, scratch = [], []
    if not is_forward:
        extra = list(receivers)
        count = extra[0].shape[1]
        scratch = [
            pltpu.VMEM((256, count), jnp.bfloat16),
            pltpu.VMEM((384, count), jnp.bfloat16),
            pltpu.VMEM((2, 256, 128), jnp.float32),
        ]
    return pl.pallas_call(
        functools.partial(pack_kernel, is_forward),
        out_shape=out,
        in_specs=[SMEM_SPEC] + [hbm] * 4 + [VMEM_SPEC] * len(extra),
        out_specs=tuple(VMEM_SPEC for _ in out),
        scratch_shapes=[
            pltpu.VMEM((2, 2, 3, 2, 64 + 2 * PAD, 128), jnp.float32),
            pltpu.VMEM((3, 2, 3, 64, 128), jnp.float32),
            pltpu.SemaphoreType.DMA((2, 9)),
            pltpu.SemaphoreType.DMA((3, 2)),
        ]
        + scratch,
        compiler_params=pltpu.CompilerParams(vmem_limit_bytes=5 << 20),
        name="pack_forward" if is_forward else "pack_adjoint",
    )(meta, *whole, *extra)


def first_plane(meta, even, odd):
    return OWN + even + lax.rem(meta[0], 2) * (odd - even)


def load_mats(lam, mu, buoy, mats):
    def own(p):
        for i, array in enumerate((buoy, lam, mu)):
            mats[i, p + OWN] = SCALES[i] * array[p]

    planes(0, 8, own)


def load_halo(ref, rightward, w_both, mats):
    for shot in range(2):
        for i, (field, slot, _) in enumerate(RIGHTWARD if rightward else LEFTWARD):
            w_both[field][shot, slot, pl.ds(PAD, 64), :] = ref[SENT * shot + i]
    if mats is not None:
        for i, (which, _, slot) in enumerate(MATS_RIGHTWARD if rightward else MATS_LEFTWARD):
            mats[which, slot] = SCALES[which] * ref[2 * SENT + i]


def load_chip_halo(meta, ref, w_both, mats):
    odd = lax.rem(meta[0], 2) == 1

    @pl.when(odd)
    def _():
        load_halo(ref, True, w_both, mats)

    @pl.when(jnp.logical_not(odd))
    def _():
        load_halo(ref, False, w_both, mats)


def load_cross_halo(meta, ref, w_both, mats):
    odd = lax.rem(meta[0], 2) == 1

    @pl.when(odd)
    def _():
        load_halo(ref, False, w_both, mats)

    @pl.when(jnp.logical_not(odd))
    def _():
        load_halo(ref, True, w_both, mats)


NEAR = ((1, 0, 8), (8, -1, 1), (1, 0, 7), (2, -1, 8), (8, -1, 1), (2, 0, 6), (3, 0, 6), (3, 0, 5))
FAR = ((0, 8, 1), (-1, 8, 1), (0, 7, 1), (-1, 7, 3), (-1, 8, 1), (0, 6, 2), (0, 6, 3), (0, 5, 3))
NEAR_SOURCES = ((1, -2, 9), (2, -1, 7))
FAR_SOURCES = ((-2, 7, 3), (-1, 6, 3))


def forward_passes(meta, src_index, src_amp, w_both, mats, strains, passes, sources):
    kb = lambda q, flat: mats[0, q, flat, :]
    slabs = [of_shot(w_both, shot) for shot in range(2)]

    def own(moment, stress, q):
        for shot, u in enumerate(slabs):
            for begin in range(0, 64, CHUNK):
                strain = strain_chunk(u, q, begin)
                for i, value in enumerate(strain):
                    strains[shot, moment, i, q - OWN, pl.ds(begin, CHUNK), :] = value
                if stress:
                    stress_chunk(u, mats, q, begin, strain)

    def outer(q):
        for u in slabs:
            for begin in range(0, 64, CHUNK):
                stress_chunk(u, mats, q, begin, strain_chunk(u, q, begin))

    def velocity(q):
        for u in slabs:
            velocity_plane(u, kb, q)

    def run(i, body):
        even, odd, count = passes[i]
        planes(first_plane(meta, even, odd), count, body)

    def source(moment):
        even, odd, count = sources[moment]
        low = first_plane(meta, even, odd)
        for shot, u in enumerate(slabs):
            cell = src_index[shot]
            slot = lax.shift_right_logical(cell, 13) - 8 * meta[0] + OWN
            row = jnp.bitwise_and(lax.shift_right_logical(cell, 7), 63) + PAD
            lane = jnp.bitwise_and(cell, 127)

            @pl.when(jnp.logical_and(slot >= low, slot < low + count))
            def _():
                amount = jnp.where(lanes(1) == lane, src_amp[shot, moment], 0.0)
                for field in (SXX, SYY, SZZ):
                    u[field][slot, pl.ds(row, 1), :] += amount

    run(0, velocity)
    run(1, outer)
    run(2, functools.partial(own, 0, True))
    source(0)
    run(3, velocity)
    run(4, outer)
    run(5, functools.partial(own, 1, True))
    source(1)
    run(6, velocity)
    run(7, functools.partial(own, 2, False))


def forward_near_kernel(meta, src_index, src_amp, lam, mu, buoy, chip, *rest):
    strains, mats, *w_both = rest[9:]
    load_mats(lam, mu, buoy, mats)
    load_chip_halo(meta, chip, w_both, mats)
    forward_passes(meta, src_index, src_amp, w_both, mats, strains, NEAR, NEAR_SOURCES)


def forward_far_kernel(meta, src_index, src_amp, cross, *rest):
    strains, mats, *w_both = rest[11:]
    load_cross_halo(meta, cross, w_both, mats)
    forward_passes(meta, src_index, src_amp, w_both, mats, strains, FAR, FAR_SOURCES)


def call(kernel, name, operands, out_shape, scalars, aliases=None):
    return pl.pallas_call(
        kernel,
        out_shape=out_shape,
        in_specs=[SMEM_SPEC] * scalars + [VMEM_SPEC] * (len(operands) - scalars),
        out_specs=tuple(VMEM_SPEC for _ in out_shape),
        input_output_aliases=aliases or {},
        compiler_params=pltpu.CompilerParams(vmem_limit_bytes=4 << 20),
        name=name,
    )(*operands)


def forward_near(meta, src_index, src_amp, lam, mu, buoy, chip, slabs):
    operands = (meta, src_index, src_amp, lam, mu, buoy, chip) + tuple(slabs)
    aliases = {7 + i: 2 + i for i in range(9)}
    return call(forward_near_kernel, "forward_near", operands, (STRAINS, MATS) + SLABS, 3, aliases)


def forward_far(meta, src_index, src_amp, cross, held):
    operands = (meta, src_index, src_amp, cross) + tuple(held)
    aliases = {4 + i: i for i in range(11)}
    return call(forward_far_kernel, "forward_far", operands, (STRAINS, MATS) + SLABS, 3, aliases)


def split_values(amounts, shot, cell, moments, values):
    count = cell.shape[1]
    lane = jnp.bitwise_and(cell, 127)
    lane_hot = lax.broadcasted_iota(jnp.int32, (128, count), 0) == lane
    for i, moment in enumerate(moments):
        left = amounts[moment, pl.ds(shot, 1), :]
        for part in range(3):
            piece = left.astype(jnp.bfloat16).astype(jnp.float32)
            left = left - piece
            values[pl.ds(128 * (len(moments) * part + i), 128), :] = jnp.where(
                lane_hot, piece, 0.0
            ).astype(jnp.bfloat16)


def rows_of(cell, base, first, count):
    row = lax.shift_right_logical(cell, 7) - base
    at = first + lax.broadcasted_iota(jnp.int32, (count, cell.shape[1]), 0)
    return jnp.where(at == row, 1.0, 0.0).astype(jnp.bfloat16)


def gathered(hot, values, moments):
    product = lax.dot_general(
        hot, values, (((1,), (1,)), ((), ())), preferred_element_type=jnp.float32
    )
    size = 128 * moments
    return product[:, :size] + product[:, size : 2 * size] + product[:, 2 * size :]


INJECT_FIRST = 2 * 64
INJECT_ROWS = 11 * 64


def inject_kernel(meta, cells, amounts, out, rows_hot, values):
    base = (8 * meta[0] - OWN) * 64
    for shot in range(2):
        cell = cells[pl.ds(shot, 1), :]

        def hot(k, carry):
            rows_hot[pl.ds(k * 64, 64), :] = rows_of(cell, base, INJECT_FIRST + k * 64, 64)
            return carry

        lax.fori_loop(0, INJECT_ROWS // 64, hot, 0)
        split_values(amounts, shot, cell, (0, 1, 2), values)
        size = INJECT_ROWS // 2
        for k in range(2):
            total = gathered(rows_hot[pl.ds(k * size, size), :], values[...], 3)
            for moment in range(3):
                out[shot, moment, pl.ds(INJECT_FIRST + k * size, size), :] = total[
                    :, 128 * moment : 128 * moment + 128
                ]


def inject(meta, cells, amounts):
    count = cells.shape[1]
    vmem = pl.BlockSpec(memory_space=pltpu.VMEM)
    return pl.pallas_call(
        inject_kernel,
        out_shape=jax.ShapeDtypeStruct((2, 3, SLOTS * 64, 128), jnp.float32),
        in_specs=[pl.BlockSpec(memory_space=pltpu.SMEM), vmem, vmem],
        out_specs=vmem,
        scratch_shapes=[
            pltpu.VMEM((INJECT_ROWS, count), jnp.bfloat16),
            pltpu.VMEM((3 * 384, count), jnp.bfloat16),
        ],
        compiler_params=pltpu.CompilerParams(vmem_limit_bytes=12 << 20),
        name="receivers",
    )(meta, cells, amounts)


def adjoint_passes(meta, w_both, mats, strains, dense, grads, passes):
    kb = lambda q, flat: -mats[0, q, flat, :]
    slabs = [of_shot(w_both, shot) for shot in range(2)]

    def own(moment, stress, q):
        p = q - OWN
        for begin in range(0, 64, CHUNK):
            flat = pl.ds(begin, CHUNK)
            if moment < 2:
                bulk, shear = grads[0, p, flat, :], grads[1, p, flat, :]
            else:
                bulk, shear = 0.0, 0.0
            for shot, w in enumerate(slabs):
                exx, eyy, ezz, eyz, exz, exy = strain_chunk(w, q, begin)
                fxx, fyy, fzz, fyz, fxz, fxy = [
                    strains[shot, moment, i, p, flat, :] for i in range(6)
                ]
                bulk = bulk + (fxx + fyy + fzz) * (exx + eyy + ezz)
                shear = shear + (
                    2.0 * (fxx * exx + fyy * eyy + fzz * ezz)
                    + (fyz * eyz + fxz * exz + fxy * exy)
                )
                if stress:
                    stress_chunk(w, mats, q, begin, (exx, eyy, ezz, eyz, exz, exy), -1.0)
            grads[0, p, flat, :] = bulk
            grads[1, p, flat, :] = shear

    def outer(q):
        for w in slabs:
            for begin in range(0, 64, CHUNK):
                stress_chunk(w, mats, q, begin, strain_chunk(w, q, begin), -1.0)

    def velocity(moment, q):
        for shot, w in enumerate(slabs):
            velocity_plane(w, kb, q, dense.at[shot, moment])

    def run(i, body):
        even, odd, count = passes[i]
        planes(first_plane(meta, even, odd), count, body)

    run(0, functools.partial(velocity, 2))
    run(1, outer)
    run(2, functools.partial(own, 2, True))
    run(3, functools.partial(velocity, 1))
    run(4, outer)
    run(5, functools.partial(own, 1, True))
    run(6, functools.partial(velocity, 0))
    run(7, functools.partial(own, 0, False))


def give_away(meta, grads, give, passes):
    even, odd, count = passes[7]
    low = first_plane(meta, even, odd) - OWN
    rows = pl.ds(pl.multiple_of(32 - 32 * meta[1], 32), 32)
    for i in range(2):
        for j in range(count):
            give[i, j] = grads[i, low + j, rows, :]


def adjoint_near_kernel(meta, mats, chip, strains, dense, *rest):
    give, grads, *w_both = rest[9:]
    load_chip_halo(meta, chip, w_both, None)
    adjoint_passes(meta, w_both, mats, strains, dense, grads, NEAR)
    give_away(meta, grads, give, NEAR)


def adjoint_far_kernel(meta, cross, mats, strains, dense, *rest):
    give, grads, *w_both = rest[10:]
    load_cross_halo(meta, cross, w_both, None)
    adjoint_passes(meta, w_both, mats, strains, dense, grads, FAR)
    give_away(meta, grads, give, FAR)


def gift(passes):
    return jax.ShapeDtypeStruct((2, passes[7][2], 32, 128), jnp.float32)


def adjoint_near(meta, mats, chip, strains, dense, slabs):
    operands = (meta, mats, chip, strains, dense) + tuple(slabs)
    aliases = {5 + i: 2 + i for i in range(9)}
    out = (gift(NEAR), GRADS) + SLABS
    return call(adjoint_near_kernel, "adjoint_near", operands, out, 1, aliases)


def adjoint_far(meta, cross, mats, strains, dense, held):
    operands = (meta, cross, mats, strains, dense) + tuple(held)
    aliases = {5 + i: 1 + i for i in range(10)}
    out = (gift(FAR), GRADS) + SLABS
    return call(adjoint_far_kernel, "adjoint_far", operands, out, 1, aliases)


def finish_kernel(meta, grads, near, far, out_lambda, out_shear):
    rows = pl.ds(pl.multiple_of(32 * meta[1], 32), 32)
    for ref, passes in ((near, NEAR), (far, FAR)):
        even, odd, count = passes[7]
        low = first_plane(meta, even, odd) - OWN
        for i, out in enumerate((out_lambda, out_shear)):
            for j in range(count):
                out[low + j] = grads[i, low + j, rows, :] + ref[i, j]


def finish(meta, grads, near, far):
    out = jax.ShapeDtypeStruct((8, 32, 128), jnp.float32)
    return call(finish_kernel, "finish", (meta, grads, near, far), (out, out), 1)


def shards(
    lame_lambda, lame_shear, buoyancy, fwd_state, adj_state, src_index, src_amp, recv_index, residual
):
    count = lax.axis_size("space")
    onchip = [(i, i + 1) for i in range(0, count, 2)] + [(i + 1, i) for i in range(0, count, 2)]
    between = [(i, i + 1) for i in range(1, count - 1, 2)]
    between = between + [(j, i) for i, j in between]
    swap_chips = lambda x: lax.ppermute(x, "space", between)
    swap_cores = lambda x: lax.ppermute(x, "space", onchip)
    meta = jnp.stack([lax.axis_index("space"), lax.axis_index("shot")]).astype(jnp.int32)
    mats = (lame_lambda, lame_shear, buoyancy)
    swap_shots = lambda x: lax.ppermute(x, "shot", [(0, 1), (1, 0)])
    amounts = residual.transpose(1, 0, 2)
    f_cross, f_chip, *f_slabs = pack(meta, fwd_state, *mats, None)
    f_cross = swap_chips(f_cross)
    a_cross, a_chip, *a_slabs = pack(meta, adj_state, *mats, (recv_index, amounts))
    a_cross = swap_chips(a_cross)
    f_chip = swap_cores(f_chip)
    dense = inject(meta, recv_index, amounts).reshape(2, 3, SLOTS, 64, 128)
    a_chip = swap_cores(a_chip)
    held = forward_near(meta, src_index, src_amp, *mats, f_chip, f_slabs)
    strains, scaled, *_ = forward_far(meta, src_index, src_amp, f_cross, held)
    near, *held = adjoint_near(meta, scaled, a_chip, strains, dense, a_slabs)
    near = swap_shots(near)
    far, grads, *_ = adjoint_far(meta, a_cross, scaled, strains, dense, held)
    far = swap_shots(far)
    return tuple(finish(meta, grads, near, far))


def solution(mesh):
    in_specs = (
        P("space", None, None),
        P("space", None, None),
        P("space", None, None),
        P(None, "shot", "space", None, None),
        P(None, "shot", "space", None, None),
        P("shot"),
        P("shot", None),
        P("shot", None),
        P("shot", None, None),
    )
    out_specs = (P("space", "shot", None), P("space", "shot", None))
    return jax.shard_map(shards, mesh=mesh, in_specs=in_specs, out_specs=out_specs, check_vma=False)
```

```python
import functools

import jax
import jax.numpy as jnp
from jax import lax
from jax.experimental import pallas as pl
from jax.experimental.pallas import tpu as pltpu
from jax.sharding import PartitionSpec as P

courant = 0.2
VX, VY, VZ, SXX, SYY, SZZ, SYZ, SXZ, SXY = range(9)

SLOTS = 14
OWN = 3
PAD = 8

NORMAL_X = (SXX, SXZ, SXY)
STRESSES = (SXX, SYY, SZZ, SYZ, SXZ, SXY)
RIGHTWARD = (
    ((VX, 1, "second"), (VX, 2, "raw"), (VY, 2, "second"), (VZ, 2, "second"))
    + tuple((field, 1, "fresh") for field in NORMAL_X)
    + tuple((field, 2, "raw") for field in STRESSES)
)
LEFTWARD = (
    ((VX, 11, "first"), (VY, 11, "raw"), (VY, 12, "first"), (VZ, 11, "raw"), (VZ, 12, "first"))
    + tuple((field, 11, "raw") for field in STRESSES)
    + tuple((field, 12, "fresh") for field in STRESSES)
)
MATS_RIGHTWARD = ((0, 6, 1), (0, 7, 2), (1, 7, 2), (2, 7, 2))
MATS_LEFTWARD = ((0, 0, 11), (0, 1, 12), (1, 0, 11), (2, 0, 11))
SENT = 17
SCALES = (courant, courant, 2.0 * courant)
VMEM_SPEC = pl.BlockSpec(memory_space=pltpu.VMEM)
SMEM_SPEC = pl.BlockSpec(memory_space=pltpu.SMEM)
SLABS = (jax.ShapeDtypeStruct((2, SLOTS, 64 + 2 * PAD, 128), jnp.float32),) * 9
STRAINS = jax.ShapeDtypeStruct((2, 3, 6, 8, 64, 128), jnp.float32)
MATS = jax.ShapeDtypeStruct((3, SLOTS, 64, 128), jnp.float32)
GRADS = jax.ShapeDtypeStruct((2, 8, 64, 128), jnp.float32)
CHUNK = 16


def of_shot(w, shot):
    return [ref.at[shot] for ref in w]


def lanes(rows):
    return lax.broadcasted_iota(jnp.int32, (rows, 128), 1)


def below_z(x):
    return jnp.where(lanes(x.shape[0]) == 0, 0.0, pltpu.roll(x, 1, 1))


def above_z(x):
    return jnp.where(lanes(x.shape[0]) == 127, 0.0, pltpu.roll(x, 127, 1))


def velocity_plane(w, kb, q, inject=None):
    for start in range(0, 64, CHUNK):
        at = pl.ds(PAD + start, CHUNK)
        down = pl.ds(PAD + start - 1, CHUNK)
        up = pl.ds(PAD + start + 1, CHUNK)
        flat = pl.ds(start, CHUNK)
        xy_b, xz_b = w[SXY][q - 1, at, :], w[SXZ][q - 1, at, :]
        new_x = w[VX][q - 1, at, :] + kb(q - 1, flat) * (
            (w[SXX][q, at, :] - w[SXX][q - 1, at, :])
            + (xy_b - w[SXY][q - 1, down, :])
            + (xz_b - below_z(xz_b))
        )
        yz, zz = w[SYZ][q, at, :], w[SZZ][q, at, :]
        scaled = kb(q, flat)
        new_y = w[VY][q, at, :] + scaled * (
            (w[SXY][q, at, :] - xy_b) + (w[SYY][q, up, :] - w[SYY][q, at, :]) + (yz - below_z(yz))
        )
        new_z = w[VZ][q, at, :] + scaled * (
            (w[SXZ][q, at, :] - xz_b) + (yz - w[SYZ][q, down, :]) + (above_z(zz) - zz)
        )
        if inject is not None:
            new_z = new_z + inject[q, flat, :]
        w[VX][q - 1, at, :] = new_x
        w[VY][q, at, :] = new_y
        w[VZ][q, at, :] = new_z


def strain_chunk(w, q, start):
    at = pl.ds(PAD + start, CHUNK)
    down = pl.ds(PAD + start - 1, CHUNK)
    up = pl.ds(PAD + start + 1, CHUNK)
    vx, vy, vz = w[VX][q, at, :], w[VY][q, at, :], w[VZ][q, at, :]
    exx = vx - w[VX][q - 1, at, :]
    eyy = vy - w[VY][q, down, :]
    ezz = vz - below_z(vz)
    eyz = (above_z(vy) - vy) + (w[VZ][q, up, :] - vz)
    exz = (above_z(vx) - vx) + (w[VZ][q + 1, at, :] - vz)
    exy = (w[VX][q, up, :] - vx) + (w[VY][q + 1, at, :] - vy)
    return exx, eyy, ezz, eyz, exz, exy


def stress_chunk(w, mats, q, start, strain, sign=1.0):
    at = pl.ds(PAD + start, CHUNK)
    flat = pl.ds(start, CHUNK)
    exx, eyy, ezz, eyz, exz, exy = strain
    twice = mats[2, q, flat, :]
    bulk = mats[1, q, flat, :] * (exx + eyy + ezz)
    once = 0.5 * twice
    for field, change in (
        (SXX, bulk + twice * exx),
        (SYY, bulk + twice * eyy),
        (SZZ, bulk + twice * ezz),
        (SYZ, once * eyz),
        (SXZ, once * exz),
        (SXY, once * exy),
    ):
        old = w[field][q, at, :]
        w[field][q, at, :] = old + change if sign > 0 else old - change


UNROLL = 4


def planes(low, count, body):
    whole = count // UNROLL

    def step(i, carry):
        for j in range(UNROLL):
            body(low + UNROLL * i + j)
        return carry

    if whole > 1:
        lax.fori_loop(0, whole, step, 0)
    else:
        for j in range(whole * UNROLL):
            body(low + j)
    for j in range(whole * UNROLL, count):
        body(low + j)


def clear_edges(w, slots):
    zero = jnp.zeros((PAD, 128), jnp.float32)
    for field, top in ((VX, 1), (VY, 0), (VZ, 1), (SXY, 0), (SYY, 1), (SYZ, 0)):
        for slot in range(slots):
            w[field][slot, pl.ds(PAD + 64 if top else 0, PAD), :] = zero


def early_velocities(w, shot, scaled, q, begin):
    at = pl.ds(PAD + begin, CHUNK)
    down = pl.ds(PAD + begin - 1, CHUNK)
    up = pl.ds(PAD + begin + 1, CHUNK)
    xy_b, xz_b = w[SXY][shot, q - 1, at, :], w[SXZ][shot, q - 1, at, :]
    new_x = w[VX][shot, q - 1, at, :] + scaled(q - 1) * (
        (w[SXX][shot, q, at, :] - w[SXX][shot, q - 1, at, :])
        + (xy_b - w[SXY][shot, q - 1, down, :])
        + (xz_b - below_z(xz_b))
    )
    yz, zz = w[SYZ][shot, q, at, :], w[SZZ][shot, q, at, :]
    new_y = w[VY][shot, q, at, :] + scaled(q) * (
        (w[SXY][shot, q, at, :] - xy_b)
        + (w[SYY][shot, q, up, :] - w[SYY][shot, q, at, :])
        + (yz - below_z(yz))
    )
    new_z = w[VZ][shot, q, at, :] + scaled(q) * (
        (w[SXZ][shot, q, at, :] - xz_b) + (yz - w[SYZ][shot, q, down, :]) + (above_z(zz) - zz)
    )
    return new_x, new_y, new_z


def pack_kernel(is_forward, meta, state, lam, mu, buoy, *rest):
    if is_forward:
        cross, chip, *w, early, edge, sems, edge_sems = rest
    else:
        cells, amounts, cross, chip, *w, early, edge, sems, edge_sems, hot, values, dense = rest
    odd = lax.rem(meta[0], 2) == 1
    edges = []
    for i, array in enumerate((buoy, lam, mu)):
        for side, first in ((0, 0), (1, 5)):
            edges.append(
                pltpu.make_async_copy(
                    array.at[pl.ds(first, 3)], edge.at[i, side], edge_sems.at[i, side]
                )
            )
    loads = [
        [
            pltpu.make_async_copy(
                state.at[field, shot],
                w[field].at[shot, pl.ds(OWN, 8), pl.ds(PAD, 64)],
                sems.at[shot, field],
            )
            for field in range(9)
        ]
        for shot in range(2)
    ]
    for load in edges + loads[0] + loads[1]:
        load.start()
    for shot in range(2):
        clear_edges(of_shot(w, shot), SLOTS)
    zero = jnp.zeros((PAD, 128), jnp.float32)
    for shot in range(2):
        for side in range(2):
            for field, row in ((VX, PAD + 64), (VY, 0), (VZ, PAD + 64)):
                for slot in range(2):
                    early[shot, side, field, slot, pl.ds(row, PAD), :] = zero
    if not is_forward:
        base = (8 * meta[0] - OWN) * 64
        for shot in range(2):
            cell = cells[pl.ds(shot, 1), :]
            for i, plane in enumerate((1, 2, 6, 7)):
                hot[pl.ds(64 * i, 64), :] = rows_of(cell, base, (plane + OWN) * 64, 64)
            split_values(amounts, shot, cell, (2,), values)
            dense[shot] = gathered(hot[...], values[...], 1)
    for load in edges:
        load.wait()
    factor = courant if is_forward else -courant

    def send(to_cross):
        for shot in range(2):
            for load in loads[shot]:
                load.wait()
            for side, table in ((1, RIGHTWARD), (0, LEFTWARD)):
                target = cross if side == to_cross else chip
                plane = 6 if side == 1 else 1
                new = early.at[shot, side]
                for j in range(2):
                    q = OWN + plane + j
                    for begin in range(0, 64, CHUNK):
                        at, flat = pl.ds(PAD + begin, CHUNK), pl.ds(begin, CHUNK)
                        scaled = lambda q: factor * edge[0, side, q - OWN - 5 * side, flat, :]
                        new_x, new_y, new_z = early_velocities(w, shot, scaled, q, begin)
                        if not is_forward:
                            row = 64 * (2 * side + j) + begin
                            new_z = new_z + dense[shot, pl.ds(row, CHUNK), :]
                        new[VX, j, at, :] = new_x
                        new[VY, j, at, :] = new_y
                        new[VZ, j, at, :] = new_z
                for begin in range(0, 64, CHUNK):
                    at, flat = pl.ds(PAD + begin, CHUNK), pl.ds(begin, CHUNK)
                    down, up = pl.ds(PAD + begin - 1, CHUNK), pl.ds(PAD + begin + 1, CHUNK)
                    vx, vy, vz = new[VX, 1, at, :], new[VY, 0, at, :], new[VZ, 0, at, :]
                    exx = vx - new[VX, 0, at, :]
                    eyy = vy - new[VY, 0, down, :]
                    ezz = vz - below_z(vz)
                    eyz = (above_z(vy) - vy) + (new[VZ, 0, up, :] - vz)
                    exz = (above_z(vx) - vx) + (new[VZ, 1, at, :] - vz)
                    exy = (new[VX, 1, up, :] - vx) + (new[VY, 1, at, :] - vy)
                    once = factor * edge[2, side, plane - 5 * side, flat, :]
                    twice = 2.0 * once
                    bulk = (factor * edge[1, side, plane - 5 * side, flat, :]) * (exx + eyy + ezz)
                    change = {
                        SXX: bulk + twice * exx,
                        SYY: bulk + twice * eyy,
                        SZZ: bulk + twice * ezz,
                        SYZ: once * eyz,
                        SXZ: once * exz,
                        SXY: once * exy,
                    }
                    for i, (field, _, kind) in enumerate(table):
                        if kind == "raw":
                            value = w[field][shot, OWN + 7 * side, at, :]
                        elif kind == "fresh":
                            value = w[field][shot, OWN + plane, at, :] + change[field]
                        else:
                            value = new[field, 0 if kind == "first" else 1, at, :]
                        target[SENT * shot + i, flat, :] = value
        if is_forward:
            for side, mats in ((1, MATS_RIGHTWARD), (0, MATS_LEFTWARD)):
                target = cross if side == to_cross else chip
                for i, (which, own, _) in enumerate(mats):
                    target[2 * SENT + i] = edge[which, side, own - 5 * side]

    @pl.when(odd)
    def _():
        send(1)

    @pl.when(jnp.logical_not(odd))
    def _():
        send(0)


def pack(meta, state, lam, mu, buoy, receivers):
    hbm = pl.BlockSpec(memory_space=pltpu.HBM)
    is_forward = receivers is None
    big = jax.ShapeDtypeStruct((2 * SENT + (4 if is_forward else 0), 64, 128), jnp.float32)
    out = (big, big) + SLABS
    whole = [pltpu.with_memory_space_constraint(x, pltpu.HBM) for x in (state, lam, mu, buoy)]
    extra, scratch = [], []
    if not is_forward:
        extra = list(receivers)
        count = extra[0].shape[1]
        scratch = [
            pltpu.VMEM((256, count), jnp.bfloat16),
            pltpu.VMEM((384, count), jnp.bfloat16),
            pltpu.VMEM((2, 256, 128), jnp.float32),
        ]
    return pl.pallas_call(
        functools.partial(pack_kernel, is_forward),
        out_shape=out,
        in_specs=[SMEM_SPEC] + [hbm] * 4 + [VMEM_SPEC] * len(extra),
        out_specs=tuple(VMEM_SPEC for _ in out),
        scratch_shapes=[
            pltpu.VMEM((2, 2, 3, 2, 64 + 2 * PAD, 128), jnp.float32),
            pltpu.VMEM((3, 2, 3, 64, 128), jnp.float32),
            pltpu.SemaphoreType.DMA((2, 9)),
            pltpu.SemaphoreType.DMA((3, 2)),
        ]
        + scratch,
        compiler_params=pltpu.CompilerParams(vmem_limit_bytes=5 << 20),
        name="pack_forward" if is_forward else "pack_adjoint",
    )(meta, *whole, *extra)


def first_plane(meta, even, odd):
    return OWN + even + lax.rem(meta[0], 2) * (odd - even)


def load_mats(lam, mu, buoy, mats):
    def own(p):
        for i, array in enumerate((buoy, lam, mu)):
            mats[i, p + OWN] = SCALES[i] * array[p]

    planes(0, 8, own)


def load_halo(ref, rightward, w_both, mats):
    for shot in range(2):
        for i, (field, slot, _) in enumerate(RIGHTWARD if rightward else LEFTWARD):
            w_both[field][shot, slot, pl.ds(PAD, 64), :] = ref[SENT * shot + i]
    if mats is not None:
        for i, (which, _, slot) in enumerate(MATS_RIGHTWARD if rightward else MATS_LEFTWARD):
            mats[which, slot] = SCALES[which] * ref[2 * SENT + i]


def load_chip_halo(meta, ref, w_both, mats):
    odd = lax.rem(meta[0], 2) == 1

    @pl.when(odd)
    def _():
        load_halo(ref, True, w_both, mats)

    @pl.when(jnp.logical_not(odd))
    def _():
        load_halo(ref, False, w_both, mats)


def load_cross_halo(meta, ref, w_both, mats):
    odd = lax.rem(meta[0], 2) == 1

    @pl.when(odd)
    def _():
        load_halo(ref, False, w_both, mats)

    @pl.when(jnp.logical_not(odd))
    def _():
        load_halo(ref, True, w_both, mats)


NEAR = ((1, 0, 8), (8, -1, 1), (1, 0, 7), (2, -1, 8), (8, -1, 1), (2, 0, 6), (3, 0, 6), (3, 0, 5))
FAR = ((0, 8, 1), (-1, 8, 1), (0, 7, 1), (-1, 7, 3), (-1, 8, 1), (0, 6, 2), (0, 6, 3), (0, 5, 3))
NEAR_SOURCES = ((1, -2, 9), (2, -1, 7))
FAR_SOURCES = ((-2, 7, 3), (-1, 6, 3))


def forward_passes(meta, src_index, src_amp, w_both, mats, strains, passes, sources):
    kb = lambda q, flat: mats[0, q, flat, :]
    slabs = [of_shot(w_both, shot) for shot in range(2)]

    def own(moment, stress, q):
        for shot, u in enumerate(slabs):
            for begin in range(0, 64, CHUNK):
                strain = strain_chunk(u, q, begin)
                for i, value in enumerate(strain):
                    strains[shot, moment, i, q - OWN, pl.ds(begin, CHUNK), :] = value
                if stress:
                    stress_chunk(u, mats, q, begin, strain)

    def outer(q):
        for u in slabs:
            for begin in range(0, 64, CHUNK):
                stress_chunk(u, mats, q, begin, strain_chunk(u, q, begin))

    def velocity(q):
        for u in slabs:
            velocity_plane(u, kb, q)

    def run(i, body):
        even, odd, count = passes[i]
        planes(first_plane(meta, even, odd), count, body)

    def source(moment):
        even, odd, count = sources[moment]
        low = first_plane(meta, even, odd)
        for shot, u in enumerate(slabs):
            cell = src_index[shot]
            slot = lax.shift_right_logical(cell, 13) - 8 * meta[0] + OWN
            row = jnp.bitwise_and(lax.shift_right_logical(cell, 7), 63) + PAD
            lane = jnp.bitwise_and(cell, 127)

            @pl.when(jnp.logical_and(slot >= low, slot < low + count))
            def _():
                amount = jnp.where(lanes(1) == lane, src_amp[shot, moment], 0.0)
                for field in (SXX, SYY, SZZ):
                    u[field][slot, pl.ds(row, 1), :] += amount

    run(0, velocity)
    run(1, outer)
    run(2, functools.partial(own, 0, True))
    source(0)
    run(3, velocity)
    run(4, outer)
    run(5, functools.partial(own, 1, True))
    source(1)
    run(6, velocity)
    run(7, functools.partial(own, 2, False))


def forward_near_kernel(meta, src_index, src_amp, lam, mu, buoy, chip, *rest):
    strains, mats, *w_both = rest[9:]
    load_mats(lam, mu, buoy, mats)
    load_chip_halo(meta, chip, w_both, mats)
    forward_passes(meta, src_index, src_amp, w_both, mats, strains, NEAR, NEAR_SOURCES)


def forward_far_kernel(meta, src_index, src_amp, cross, *rest):
    strains, mats, *w_both = rest[11:]
    load_cross_halo(meta, cross, w_both, mats)
    forward_passes(meta, src_index, src_amp, w_both, mats, strains, FAR, FAR_SOURCES)


def call(kernel, name, operands, out_shape, scalars, aliases=None):
    return pl.pallas_call(
        kernel,
        out_shape=out_shape,
        in_specs=[SMEM_SPEC] * scalars + [VMEM_SPEC] * (len(operands) - scalars),
        out_specs=tuple(VMEM_SPEC for _ in out_shape),
        input_output_aliases=aliases or {},
        compiler_params=pltpu.CompilerParams(vmem_limit_bytes=4 << 20),
        name=name,
    )(*operands)


def forward_near(meta, src_index, src_amp, lam, mu, buoy, chip, slabs):
    operands = (meta, src_index, src_amp, lam, mu, buoy, chip) + tuple(slabs)
    aliases = {7 + i: 2 + i for i in range(9)}
    return call(forward_near_kernel, "forward_near", operands, (STRAINS, MATS) + SLABS, 3, aliases)


def forward_far(meta, src_index, src_amp, cross, held):
    operands = (meta, src_index, src_amp, cross) + tuple(held)
    aliases = {4 + i: i for i in range(11)}
    return call(forward_far_kernel, "forward_far", operands, (STRAINS, MATS) + SLABS, 3, aliases)


def split_values(amounts, shot, cell, moments, values):
    count = cell.shape[1]
    lane = jnp.bitwise_and(cell, 127)
    lane_hot = lax.broadcasted_iota(jnp.int32, (128, count), 0) == lane
    for i, moment in enumerate(moments):
        left = amounts[moment, pl.ds(shot, 1), :]
        for part in range(3):
            piece = left.astype(jnp.bfloat16).astype(jnp.float32)
            left = left - piece
            values[pl.ds(128 * (len(moments) * part + i), 128), :] = jnp.where(
                lane_hot, piece, 0.0
            ).astype(jnp.bfloat16)


def rows_of(cell, base, first, count):
    row = lax.shift_right_logical(cell, 7) - base
    at = first + lax.broadcasted_iota(jnp.int32, (count, cell.shape[1]), 0)
    return jnp.where(at == row, 1.0, 0.0).astype(jnp.bfloat16)


def gathered(hot, values, moments):
    product = lax.dot_general(
        hot, values, (((1,), (1,)), ((), ())), preferred_element_type=jnp.float32
    )
    size = 128 * moments
    return product[:, :size] + product[:, size : 2 * size] + product[:, 2 * size :]


INJECT_FIRST = 2 * 64
INJECT_ROWS = 11 * 64
GROUP = 128


def ordinal(inside):
    groups = inside.shape[1] // 128
    rows = jnp.concatenate([inside[:, 128 * i : 128 * i + 128] for i in range(groups)], axis=0)
    upper = lax.broadcasted_iota(jnp.int32, (128, 128), 0) <= lax.broadcasted_iota(
        jnp.int32, (128, 128), 1
    )
    within = jnp.dot(
        rows.astype(jnp.bfloat16),
        jnp.where(upper, 1.0, 0.0).astype(jnp.bfloat16),
        preferred_element_type=jnp.float32,
    )
    result = []
    total = jnp.zeros((1, 1), jnp.float32)
    for i in range(groups):
        row = within[i : i + 1, :] + total
        result.append(row)
        total = row[:, 127:128]
    return jnp.concatenate(result, axis=1)


def inject_kernel(meta, cells, amounts, out, data, rank_ref, sizes):
    base = (8 * meta[0] - OWN) * 64
    dims = (((1,), (1,)), ((), ()))
    count = cells.shape[1]
    for shot in range(2):
        cell = cells[pl.ds(shot, 1), :]
        row = lax.shift_right_logical(cell, 7) - base - INJECT_FIRST
        inside = jnp.logical_and(row >= 0, row < INJECT_ROWS)
        rank = ordinal(jnp.where(inside, 1.0, 0.0))
        rank_ref[pl.ds(shot, 1), :] = jnp.where(inside, rank, 0.0)
        sizes[shot] = rank[0, count - 1].astype(jnp.int32)
        row = jnp.where(inside, row, 0)
        parts = [
            lax.shift_right_logical(row, 4).astype(jnp.float32),
            jnp.bitwise_and(row, 15).astype(jnp.float32),
            jnp.bitwise_and(cell, 127).astype(jnp.float32),
        ]
        for moment in range(3):
            left = amounts[moment, pl.ds(shot, 1), :]
            for part in range(3):
                piece = left.astype(jnp.bfloat16).astype(jnp.float32)
                left = left - piece
                parts.append(piece)
        parts = parts + [jnp.zeros_like(parts[0])] * 4
        data[shot] = jnp.concatenate(parts, axis=0).astype(jnp.bfloat16)

    for shot in range(2):

        def group(k, carry, first=False):
            wanted = GROUP * k + 1 + lax.broadcasted_iota(jnp.int32, (GROUP, count), 0)
            chosen = wanted.astype(jnp.float32) == rank_ref[pl.ds(shot, 1), :]
            few = lax.dot_general(
                data[shot],
                jnp.where(chosen, 1.0, 0.0).astype(jnp.bfloat16),
                dims,
                preferred_element_type=jnp.float32,
            )
            used = GROUP * k + lax.broadcasted_iota(jnp.int32, (1, GROUP), 1) < sizes[shot]
            row = jnp.where(used, 16.0 * few[0:1, :] + few[1:2, :], -1.0).astype(jnp.int32)
            lane = few[2:3, :].astype(jnp.int32)
            lane_hot = lax.broadcasted_iota(jnp.int32, (128, GROUP), 0) == lane
            values = jnp.concatenate(
                [
                    jnp.where(lane_hot, few[3 + 3 * moment + part : 4 + 3 * moment + part, :], 0.0)
                    for part in range(3)
                    for moment in range(3)
                ],
                axis=0,
            ).astype(jnp.bfloat16)
            size = INJECT_ROWS // 2
            for i in range(2):
                at = i * size + lax.broadcasted_iota(jnp.int32, (size, GROUP), 0)
                total = gathered(
                    jnp.where(at == row, 1.0, 0.0).astype(jnp.bfloat16), values, 3
                )
                place = pl.ds(INJECT_FIRST + i * size, size)
                for moment in range(3):
                    part = total[:, 128 * moment : 128 * moment + 128]

                    if first:
                        out[shot, moment, place, :] = part
                    else:
                        out[shot, moment, place, :] += part

            return carry

        groups = lax.div(sizes[shot] + GROUP - 1, GROUP)
        group(0, 0, True)
        lax.fori_loop(1, groups, group, 0)


def inject(meta, cells, amounts):
    count = cells.shape[1]
    vmem = pl.BlockSpec(memory_space=pltpu.VMEM)
    return pl.pallas_call(
        inject_kernel,
        out_shape=jax.ShapeDtypeStruct((2, 3, SLOTS * 64, 128), jnp.float32),
        in_specs=[pl.BlockSpec(memory_space=pltpu.SMEM), vmem, vmem],
        out_specs=vmem,
        scratch_shapes=[
            pltpu.VMEM((2, 16, count), jnp.bfloat16),
            pltpu.VMEM((2, count), jnp.float32),
            pltpu.SMEM((2,), jnp.int32),
        ],
        compiler_params=pltpu.CompilerParams(vmem_limit_bytes=12 << 20),
        name="receivers",
    )(meta, cells, amounts)


def adjoint_passes(meta, w_both, mats, strains, dense, grads, passes):
    kb = lambda q, flat: -mats[0, q, flat, :]
    slabs = [of_shot(w_both, shot) for shot in range(2)]

    def own(moment, stress, q):
        p = q - OWN
        for begin in range(0, 64, CHUNK):
            flat = pl.ds(begin, CHUNK)
            if moment < 2:
                bulk, shear = grads[0, p, flat, :], grads[1, p, flat, :]
            else:
                bulk, shear = 0.0, 0.0
            for shot, w in enumerate(slabs):
                exx, eyy, ezz, eyz, exz, exy = strain_chunk(w, q, begin)
                fxx, fyy, fzz, fyz, fxz, fxy = [
                    strains[shot, moment, i, p, flat, :] for i in range(6)
                ]
                bulk = bulk + (fxx + fyy + fzz) * (exx + eyy + ezz)
                shear = shear + (
                    2.0 * (fxx * exx + fyy * eyy + fzz * ezz)
                    + (fyz * eyz + fxz * exz + fxy * exy)
                )
                if stress:
                    stress_chunk(w, mats, q, begin, (exx, eyy, ezz, eyz, exz, exy), -1.0)
            grads[0, p, flat, :] = bulk
            grads[1, p, flat, :] = shear

    def outer(q):
        for w in slabs:
            for begin in range(0, 64, CHUNK):
                stress_chunk(w, mats, q, begin, strain_chunk(w, q, begin), -1.0)

    def velocity(moment, q):
        for shot, w in enumerate(slabs):
            velocity_plane(w, kb, q, dense.at[shot, moment])

    def run(i, body):
        even, odd, count = passes[i]
        planes(first_plane(meta, even, odd), count, body)

    run(0, functools.partial(velocity, 2))
    run(1, outer)
    run(2, functools.partial(own, 2, True))
    run(3, functools.partial(velocity, 1))
    run(4, outer)
    run(5, functools.partial(own, 1, True))
    run(6, functools.partial(velocity, 0))
    run(7, functools.partial(own, 0, False))


def give_away(meta, grads, give, passes):
    even, odd, count = passes[7]
    low = first_plane(meta, even, odd) - OWN
    rows = pl.ds(pl.multiple_of(32 - 32 * meta[1], 32), 32)
    for i in range(2):
        for j in range(count):
            give[i, j] = grads[i, low + j, rows, :]


def adjoint_near_kernel(meta, mats, chip, strains, dense, *rest):
    give, grads, *w_both = rest[9:]
    load_chip_halo(meta, chip, w_both, None)
    adjoint_passes(meta, w_both, mats, strains, dense, grads, NEAR)
    give_away(meta, grads, give, NEAR)


def adjoint_far_kernel(meta, cross, mats, strains, dense, *rest):
    give, grads, *w_both = rest[10:]
    load_cross_halo(meta, cross, w_both, None)
    adjoint_passes(meta, w_both, mats, strains, dense, grads, FAR)
    give_away(meta, grads, give, FAR)


def gift(passes):
    return jax.ShapeDtypeStruct((2, passes[7][2], 32, 128), jnp.float32)


def adjoint_near(meta, mats, chip, strains, dense, slabs):
    operands = (meta, mats, chip, strains, dense) + tuple(slabs)
    aliases = {5 + i: 2 + i for i in range(9)}
    out = (gift(NEAR), GRADS) + SLABS
    return call(adjoint_near_kernel, "adjoint_near", operands, out, 1, aliases)


def adjoint_far(meta, cross, mats, strains, dense, held):
    operands = (meta, cross, mats, strains, dense) + tuple(held)
    aliases = {5 + i: 1 + i for i in range(10)}
    out = (gift(FAR), GRADS) + SLABS
    return call(adjoint_far_kernel, "adjoint_far", operands, out, 1, aliases)


def finish_kernel(meta, grads, near, far, out_lambda, out_shear):
    rows = pl.ds(pl.multiple_of(32 * meta[1], 32), 32)
    for ref, passes in ((near, NEAR), (far, FAR)):
        even, odd, count = passes[7]
        low = first_plane(meta, even, odd) - OWN
        for i, out in enumerate((out_lambda, out_shear)):
            for j in range(count):
                out[low + j] = grads[i, low + j, rows, :] + ref[i, j]


def finish(meta, grads, near, far):
    out = jax.ShapeDtypeStruct((8, 32, 128), jnp.float32)
    return call(finish_kernel, "finish", (meta, grads, near, far), (out, out), 1)


def shards(
    lame_lambda, lame_shear, buoyancy, fwd_state, adj_state, src_index, src_amp, recv_index, residual
):
    count = lax.axis_size("space")
    onchip = [(i, i + 1) for i in range(0, count, 2)] + [(i + 1, i) for i in range(0, count, 2)]
    between = [(i, i + 1) for i in range(1, count - 1, 2)]
    between = between + [(j, i) for i, j in between]
    swap_chips = lambda x: lax.ppermute(x, "space", between)
    swap_cores = lambda x: lax.ppermute(x, "space", onchip)
    meta = jnp.stack([lax.axis_index("space"), lax.axis_index("shot")]).astype(jnp.int32)
    mats = (lame_lambda, lame_shear, buoyancy)
    swap_shots = lambda x: lax.ppermute(x, "shot", [(0, 1), (1, 0)])
    amounts = residual.transpose(1, 0, 2)
    f_cross, f_chip, *f_slabs = pack(meta, fwd_state, *mats, None)
    f_cross = swap_chips(f_cross)
    a_cross, a_chip, *a_slabs = pack(meta, adj_state, *mats, (recv_index, amounts))
    a_cross = swap_chips(a_cross)
    f_chip = swap_cores(f_chip)
    dense = inject(meta, recv_index, amounts).reshape(2, 3, SLOTS, 64, 128)
    a_chip = swap_cores(a_chip)
    held = forward_near(meta, src_index, src_amp, *mats, f_chip, f_slabs)
    strains, scaled, *_ = forward_far(meta, src_index, src_amp, f_cross, held)
    near, *held = adjoint_near(meta, scaled, a_chip, strains, dense, a_slabs)
    near = swap_shots(near)
    far, grads, *_ = adjoint_far(meta, a_cross, scaled, strains, dense, held)
    far = swap_shots(far)
    return tuple(finish(meta, grads, near, far))


def solution(mesh):
    in_specs = (
        P("space", None, None),
        P("space", None, None),
        P("space", None, None),
        P(None, "shot", "space", None, None),
        P(None, "shot", "space", None, None),
        P("shot"),
        P("shot", None),
        P("shot", None),
        P("shot", None, None),
    )
    out_specs = (P("space", "shot", None), P("space", "shot", None))
    return jax.shard_map(shards, mesh=mesh, in_specs=in_specs, out_specs=out_specs, check_vma=False)
```

```python
import functools

import jax
import jax.numpy as jnp
from jax import lax
from jax.experimental import pallas as pl
from jax.experimental.pallas import tpu as pltpu
from jax.sharding import PartitionSpec as P

courant = 0.2
VX, VY, VZ, SXX, SYY, SZZ, SYZ, SXZ, SXY = range(9)

SLOTS = 14
OWN = 3
PAD = 8

NORMAL_X = (SXX, SXZ, SXY)
STRESSES = (SXX, SYY, SZZ, SYZ, SXZ, SXY)
RIGHTWARD = (
    ((VX, 1, "second"), (VX, 2, "raw"), (VY, 2, "second"), (VZ, 2, "second"))
    + tuple((field, 1, "fresh") for field in NORMAL_X)
    + tuple((field, 2, "raw") for field in STRESSES)
)
LEFTWARD = (
    ((VX, 11, "first"), (VY, 11, "raw"), (VY, 12, "first"), (VZ, 11, "raw"), (VZ, 12, "first"))
    + tuple((field, 11, "raw") for field in STRESSES)
    + tuple((field, 12, "fresh") for field in STRESSES)
)
MATS_RIGHTWARD = ((0, 6, 1), (0, 7, 2), (1, 7, 2), (2, 7, 2))
MATS_LEFTWARD = ((0, 0, 11), (0, 1, 12), (1, 0, 11), (2, 0, 11))
SENT = 17
SCALES = (courant, courant, 2.0 * courant)
VMEM_SPEC = pl.BlockSpec(memory_space=pltpu.VMEM)
SMEM_SPEC = pl.BlockSpec(memory_space=pltpu.SMEM)
SLABS = (jax.ShapeDtypeStruct((2, SLOTS, 64 + 2 * PAD, 128), jnp.float32),) * 9
STRAINS = jax.ShapeDtypeStruct((2, 3, 6, 8, 64, 128), jnp.float32)
MATS = jax.ShapeDtypeStruct((3, SLOTS, 64, 128), jnp.float32)
GRADS = jax.ShapeDtypeStruct((2, 8, 64, 128), jnp.float32)
CHUNK = 32


def of_shot(w, shot):
    return [ref.at[shot] for ref in w]


def lanes(rows):
    return lax.broadcasted_iota(jnp.int32, (rows, 128), 1)


def below_z(x):
    return jnp.where(lanes(x.shape[0]) == 0, 0.0, pltpu.roll(x, 1, 1))


def above_z(x):
    return jnp.where(lanes(x.shape[0]) == 127, 0.0, pltpu.roll(x, 127, 1))


def velocity_plane(w, kb, q, inject=None):
    for start in range(0, 64, CHUNK):
        at = pl.ds(PAD + start, CHUNK)
        down = pl.ds(PAD + start - 1, CHUNK)
        up = pl.ds(PAD + start + 1, CHUNK)
        flat = pl.ds(start, CHUNK)
        xy_b, xz_b = w[SXY][q - 1, at, :], w[SXZ][q - 1, at, :]
        new_x = w[VX][q - 1, at, :] + kb(q - 1, flat) * (
            (w[SXX][q, at, :] - w[SXX][q - 1, at, :])
            + (xy_b - w[SXY][q - 1, down, :])
            + (xz_b - below_z(xz_b))
        )
        yz, zz = w[SYZ][q, at, :], w[SZZ][q, at, :]
        scaled = kb(q, flat)
        new_y = w[VY][q, at, :] + scaled * (
            (w[SXY][q, at, :] - xy_b) + (w[SYY][q, up, :] - w[SYY][q, at, :]) + (yz - below_z(yz))
        )
        new_z = w[VZ][q, at, :] + scaled * (
            (w[SXZ][q, at, :] - xz_b) + (yz - w[SYZ][q, down, :]) + (above_z(zz) - zz)
        )
        if inject is not None:
            new_z = new_z + inject[q, flat, :]
        w[VX][q - 1, at, :] = new_x
        w[VY][q, at, :] = new_y
        w[VZ][q, at, :] = new_z


def strain_chunk(w, q, start):
    at = pl.ds(PAD + start, CHUNK)
    down = pl.ds(PAD + start - 1, CHUNK)
    up = pl.ds(PAD + start + 1, CHUNK)
    vx, vy, vz = w[VX][q, at, :], w[VY][q, at, :], w[VZ][q, at, :]
    exx = vx - w[VX][q - 1, at, :]
    eyy = vy - w[VY][q, down, :]
    ezz = vz - below_z(vz)
    eyz = (above_z(vy) - vy) + (w[VZ][q, up, :] - vz)
    exz = (above_z(vx) - vx) + (w[VZ][q + 1, at, :] - vz)
    exy = (w[VX][q, up, :] - vx) + (w[VY][q + 1, at, :] - vy)
    return exx, eyy, ezz, eyz, exz, exy


def stress_chunk(w, mats, q, start, strain, sign=1.0):
    at = pl.ds(PAD + start, CHUNK)
    flat = pl.ds(start, CHUNK)
    exx, eyy, ezz, eyz, exz, exy = strain
    twice = mats[2, q, flat, :]
    bulk = mats[1, q, flat, :] * (exx + eyy + ezz)
    once = 0.5 * twice
    for field, change in (
        (SXX, bulk + twice * exx),
        (SYY, bulk + twice * eyy),
        (SZZ, bulk + twice * ezz),
        (SYZ, once * eyz),
        (SXZ, once * exz),
        (SXY, once * exy),
    ):
        old = w[field][q, at, :]
        w[field][q, at, :] = old + change if sign > 0 else old - change


UNROLL = 4


def planes(low, count, body):
    whole = count // UNROLL

    def step(i, carry):
        for j in range(UNROLL):
            body(low + UNROLL * i + j)
        return carry

    if whole > 1:
        lax.fori_loop(0, whole, step, 0)
    else:
        for j in range(whole * UNROLL):
            body(low + j)
    for j in range(whole * UNROLL, count):
        body(low + j)


def clear_edges(w, slots):
    zero = jnp.zeros((PAD, 128), jnp.float32)
    for field, top in ((VX, 1), (VY, 0), (VZ, 1), (SXY, 0), (SYY, 1), (SYZ, 0)):
        for slot in range(slots):
            w[field][slot, pl.ds(PAD + 64 if top else 0, PAD), :] = zero


def early_velocities(w, shot, scaled, q, begin):
    at = pl.ds(PAD + begin, CHUNK)
    down = pl.ds(PAD + begin - 1, CHUNK)
    up = pl.ds(PAD + begin + 1, CHUNK)
    xy_b, xz_b = w[SXY][shot, q - 1, at, :], w[SXZ][shot, q - 1, at, :]
    new_x = w[VX][shot, q - 1, at, :] + scaled(q - 1) * (
        (w[SXX][shot, q, at, :] - w[SXX][shot, q - 1, at, :])
        + (xy_b - w[SXY][shot, q - 1, down, :])
        + (xz_b - below_z(xz_b))
    )
    yz, zz = w[SYZ][shot, q, at, :], w[SZZ][shot, q, at, :]
    new_y = w[VY][shot, q, at, :] + scaled(q) * (
        (w[SXY][shot, q, at, :] - xy_b)
        + (w[SYY][shot, q, up, :] - w[SYY][shot, q, at, :])
        + (yz - below_z(yz))
    )
    new_z = w[VZ][shot, q, at, :] + scaled(q) * (
        (w[SXZ][shot, q, at, :] - xz_b) + (yz - w[SYZ][shot, q, down, :]) + (above_z(zz) - zz)
    )
    return new_x, new_y, new_z


def pack_kernel(is_forward, meta, state, lam, mu, buoy, *rest):
    if is_forward:
        cross, chip, *w, early, edge, sems, edge_sems = rest
    else:
        cells, amounts, cross, chip, *w, early, edge, sems, edge_sems, hot, values, dense = rest
    odd = lax.rem(meta[0], 2) == 1
    edges = []
    for i, array in enumerate((buoy, lam, mu)):
        for side, first in ((0, 0), (1, 5)):
            edges.append(
                pltpu.make_async_copy(
                    array.at[pl.ds(first, 3)], edge.at[i, side], edge_sems.at[i, side]
                )
            )
    loads = [
        [
            pltpu.make_async_copy(
                state.at[field, shot],
                w[field].at[shot, pl.ds(OWN, 8), pl.ds(PAD, 64)],
                sems.at[shot, field],
            )
            for field in range(9)
        ]
        for shot in range(2)
    ]
    for load in edges + loads[0] + loads[1]:
        load.start()
    for shot in range(2):
        clear_edges(of_shot(w, shot), SLOTS)
    zero = jnp.zeros((PAD, 128), jnp.float32)
    for shot in range(2):
        for side in range(2):
            for field, row in ((VX, PAD + 64), (VY, 0), (VZ, PAD + 64)):
                for slot in range(2):
                    early[shot, side, field, slot, pl.ds(row, PAD), :] = zero
    if not is_forward:
        base = (8 * meta[0] - OWN) * 64
        for shot in range(2):
            cell = cells[pl.ds(shot, 1), :]
            for i, plane in enumerate((1, 2, 6, 7)):
                hot[pl.ds(64 * i, 64), :] = rows_of(cell, base, (plane + OWN) * 64, 64)
            split_values(amounts, shot, cell, (2,), values)
            dense[shot] = gathered(hot[...], values[...], 1)
    for load in edges:
        load.wait()
    factor = courant if is_forward else -courant

    def send(to_cross):
        for shot in range(2):
            for load in loads[shot]:
                load.wait()
            for side, table in ((1, RIGHTWARD), (0, LEFTWARD)):
                target = cross if side == to_cross else chip
                plane = 6 if side == 1 else 1
                new = early.at[shot, side]
                for j in range(2):
                    q = OWN + plane + j
                    for begin in range(0, 64, CHUNK):
                        at, flat = pl.ds(PAD + begin, CHUNK), pl.ds(begin, CHUNK)
                        scaled = lambda q: factor * edge[0, side, q - OWN - 5 * side, flat, :]
                        new_x, new_y, new_z = early_velocities(w, shot, scaled, q, begin)
                        if not is_forward:
                            row = 64 * (2 * side + j) + begin
                            new_z = new_z + dense[shot, pl.ds(row, CHUNK), :]
                        new[VX, j, at, :] = new_x
                        new[VY, j, at, :] = new_y
                        new[VZ, j, at, :] = new_z
                for begin in range(0, 64, CHUNK):
                    at, flat = pl.ds(PAD + begin, CHUNK), pl.ds(begin, CHUNK)
                    down, up = pl.ds(PAD + begin - 1, CHUNK), pl.ds(PAD + begin + 1, CHUNK)
                    vx, vy, vz = new[VX, 1, at, :], new[VY, 0, at, :], new[VZ, 0, at, :]
                    exx = vx - new[VX, 0, at, :]
                    eyy = vy - new[VY, 0, down, :]
                    ezz = vz - below_z(vz)
                    eyz = (above_z(vy) - vy) + (new[VZ, 0, up, :] - vz)
                    exz = (above_z(vx) - vx) + (new[VZ, 1, at, :] - vz)
                    exy = (new[VX, 1, up, :] - vx) + (new[VY, 1, at, :] - vy)
                    once = factor * edge[2, side, plane - 5 * side, flat, :]
                    twice = 2.0 * once
                    bulk = (factor * edge[1, side, plane - 5 * side, flat, :]) * (exx + eyy + ezz)
                    change = {
                        SXX: bulk + twice * exx,
                        SYY: bulk + twice * eyy,
                        SZZ: bulk + twice * ezz,
                        SYZ: once * eyz,
                        SXZ: once * exz,
                        SXY: once * exy,
                    }
                    for i, (field, _, kind) in enumerate(table):
                        if kind == "raw":
                            value = w[field][shot, OWN + 7 * side, at, :]
                        elif kind == "fresh":
                            value = w[field][shot, OWN + plane, at, :] + change[field]
                        else:
                            value = new[field, 0 if kind == "first" else 1, at, :]
                        target[SENT * shot + i, flat, :] = value
        if is_forward:
            for side, mats in ((1, MATS_RIGHTWARD), (0, MATS_LEFTWARD)):
                target = cross if side == to_cross else chip
                for i, (which, own, _) in enumerate(mats):
                    target[2 * SENT + i] = edge[which, side, own - 5 * side]

    @pl.when(odd)
    def _():
        send(1)

    @pl.when(jnp.logical_not(odd))
    def _():
        send(0)


def pack(meta, state, lam, mu, buoy, receivers):
    hbm = pl.BlockSpec(memory_space=pltpu.HBM)
    is_forward = receivers is None
    big = jax.ShapeDtypeStruct((2 * SENT + (4 if is_forward else 0), 64, 128), jnp.float32)
    out = (big, big) + SLABS
    whole = [pltpu.with_memory_space_constraint(x, pltpu.HBM) for x in (state, lam, mu, buoy)]
    extra, scratch = [], []
    if not is_forward:
        extra = list(receivers)
        count = extra[0].shape[1]
        scratch = [
            pltpu.VMEM((256, count), jnp.bfloat16),
            pltpu.VMEM((384, count), jnp.bfloat16),
            pltpu.VMEM((2, 256, 128), jnp.float32),
        ]
    return pl.pallas_call(
        functools.partial(pack_kernel, is_forward),
        out_shape=out,
        in_specs=[SMEM_SPEC] + [hbm] * 4 + [VMEM_SPEC] * len(extra),
        out_specs=tuple(VMEM_SPEC for _ in out),
        scratch_shapes=[
            pltpu.VMEM((2, 2, 3, 2, 64 + 2 * PAD, 128), jnp.float32),
            pltpu.VMEM((3, 2, 3, 64, 128), jnp.float32),
            pltpu.SemaphoreType.DMA((2, 9)),
            pltpu.SemaphoreType.DMA((3, 2)),
        ]
        + scratch,
        compiler_params=pltpu.CompilerParams(vmem_limit_bytes=5 << 20),
        name="pack_forward" if is_forward else "pack_adjoint",
    )(meta, *whole, *extra)


def first_plane(meta, even, odd):
    return OWN + even + lax.rem(meta[0], 2) * (odd - even)


def load_mats(lam, mu, buoy, mats):
    def own(p):
        for i, array in enumerate((buoy, lam, mu)):
            mats[i, p + OWN] = SCALES[i] * array[p]

    planes(0, 8, own)


def load_halo(ref, rightward, w_both, mats):
    for shot in range(2):
        for i, (field, slot, _) in enumerate(RIGHTWARD if rightward else LEFTWARD):
            w_both[field][shot, slot, pl.ds(PAD, 64), :] = ref[SENT * shot + i]
    if mats is not None:
        for i, (which, _, slot) in enumerate(MATS_RIGHTWARD if rightward else MATS_LEFTWARD):
            mats[which, slot] = SCALES[which] * ref[2 * SENT + i]


def load_chip_halo(meta, ref, w_both, mats):
    odd = lax.rem(meta[0], 2) == 1

    @pl.when(odd)
    def _():
        load_halo(ref, True, w_both, mats)

    @pl.when(jnp.logical_not(odd))
    def _():
        load_halo(ref, False, w_both, mats)


def load_cross_halo(meta, ref, w_both, mats):
    odd = lax.rem(meta[0], 2) == 1

    @pl.when(odd)
    def _():
        load_halo(ref, False, w_both, mats)

    @pl.when(jnp.logical_not(odd))
    def _():
        load_halo(ref, True, w_both, mats)


NEAR = ((1, 0, 8), (8, -1, 1), (1, 0, 7), (2, -1, 8), (8, -1, 1), (2, 0, 6), (3, 0, 6), (3, 0, 5))
FAR = ((0, 8, 1), (-1, 8, 1), (0, 7, 1), (-1, 7, 3), (-1, 8, 1), (0, 6, 2), (0, 6, 3), (0, 5, 3))
NEAR_SOURCES = ((1, -2, 9), (2, -1, 7))
FAR_SOURCES = ((-2, 7, 3), (-1, 6, 3))


def forward_passes(meta, src_index, src_amp, w_both, mats, strains, passes, sources):
    kb = lambda q, flat: mats[0, q, flat, :]
    slabs = [of_shot(w_both, shot) for shot in range(2)]

    def own(moment, stress, q):
        for shot, u in enumerate(slabs):
            for begin in range(0, 64, CHUNK):
                strain = strain_chunk(u, q, begin)
                for i, value in enumerate(strain):
                    strains[shot, moment, i, q - OWN, pl.ds(begin, CHUNK), :] = value
                if stress:
                    stress_chunk(u, mats, q, begin, strain)

    def outer(q):
        for u in slabs:
            for begin in range(0, 64, CHUNK):
                stress_chunk(u, mats, q, begin, strain_chunk(u, q, begin))

    def velocity(q):
        for u in slabs:
            velocity_plane(u, kb, q)

    def run(i, body):
        even, odd, count = passes[i]
        planes(first_plane(meta, even, odd), count, body)

    def source(moment):
        even, odd, count = sources[moment]
        low = first_plane(meta, even, odd)
        for shot, u in enumerate(slabs):
            cell = src_index[shot]
            slot = lax.shift_right_logical(cell, 13) - 8 * meta[0] + OWN
            row = jnp.bitwise_and(lax.shift_right_logical(cell, 7), 63) + PAD
            lane = jnp.bitwise_and(cell, 127)

            @pl.when(jnp.logical_and(slot >= low, slot < low + count))
            def _():
                amount = jnp.where(lanes(1) == lane, src_amp[shot, moment], 0.0)
                for field in (SXX, SYY, SZZ):
                    u[field][slot, pl.ds(row, 1), :] += amount

    run(0, velocity)
    run(1, outer)
    run(2, functools.partial(own, 0, True))
    source(0)
    run(3, velocity)
    run(4, outer)
    run(5, functools.partial(own, 1, True))
    source(1)
    run(6, velocity)
    run(7, functools.partial(own, 2, False))


def forward_near_kernel(meta, src_index, src_amp, lam, mu, buoy, chip, *rest):
    strains, mats, *w_both = rest[9:]
    load_mats(lam, mu, buoy, mats)
    load_chip_halo(meta, chip, w_both, mats)
    forward_passes(meta, src_index, src_amp, w_both, mats, strains, NEAR, NEAR_SOURCES)


def forward_far_kernel(meta, src_index, src_amp, cross, *rest):
    strains, mats, *w_both = rest[11:]
    load_cross_halo(meta, cross, w_both, mats)
    forward_passes(meta, src_index, src_amp, w_both, mats, strains, FAR, FAR_SOURCES)


def call(kernel, name, operands, out_shape, scalars, aliases=None):
    return pl.pallas_call(
        kernel,
        out_shape=out_shape,
        in_specs=[SMEM_SPEC] * scalars + [VMEM_SPEC] * (len(operands) - scalars),
        out_specs=tuple(VMEM_SPEC for _ in out_shape),
        input_output_aliases=aliases or {},
        compiler_params=pltpu.CompilerParams(vmem_limit_bytes=4 << 20),
        name=name,
    )(*operands)


def forward_near(meta, src_index, src_amp, lam, mu, buoy, chip, slabs):
    operands = (meta, src_index, src_amp, lam, mu, buoy, chip) + tuple(slabs)
    aliases = {7 + i: 2 + i for i in range(9)}
    return call(forward_near_kernel, "forward_near", operands, (STRAINS, MATS) + SLABS, 3, aliases)


def forward_far(meta, src_index, src_amp, cross, held):
    operands = (meta, src_index, src_amp, cross) + tuple(held)
    aliases = {4 + i: i for i in range(11)}
    return call(forward_far_kernel, "forward_far", operands, (STRAINS, MATS) + SLABS, 3, aliases)


def split_values(amounts, shot, cell, moments, values):
    count = cell.shape[1]
    lane = jnp.bitwise_and(cell, 127)
    lane_hot = lax.broadcasted_iota(jnp.int32, (128, count), 0) == lane
    for i, moment in enumerate(moments):
        left = amounts[moment, pl.ds(shot, 1), :]
        for part in range(3):
            piece = left.astype(jnp.bfloat16).astype(jnp.float32)
            left = left - piece
            values[pl.ds(128 * (len(moments) * part + i), 128), :] = jnp.where(
                lane_hot, piece, 0.0
            ).astype(jnp.bfloat16)


def rows_of(cell, base, first, count):
    row = lax.shift_right_logical(cell, 7) - base
    at = first + lax.broadcasted_iota(jnp.int32, (count, cell.shape[1]), 0)
    return jnp.where(at == row, 1.0, 0.0).astype(jnp.bfloat16)


def gathered(hot, values, moments):
    product = lax.dot_general(
        hot, values, (((1,), (1,)), ((), ())), preferred_element_type=jnp.float32
    )
    size = 128 * moments
    return product[:, :size] + product[:, size : 2 * size] + product[:, 2 * size :]


INJECT_FIRST = 2 * 64
INJECT_ROWS = 11 * 64
GROUP = 128


def ordinal(inside):
    groups = inside.shape[1] // 128
    rows = jnp.concatenate([inside[:, 128 * i : 128 * i + 128] for i in range(groups)], axis=0)
    upper = lax.broadcasted_iota(jnp.int32, (128, 128), 0) <= lax.broadcasted_iota(
        jnp.int32, (128, 128), 1
    )
    within = jnp.dot(
        rows.astype(jnp.bfloat16),
        jnp.where(upper, 1.0, 0.0).astype(jnp.bfloat16),
        preferred_element_type=jnp.float32,
    )
    result = []
    total = jnp.zeros((1, 1), jnp.float32)
    for i in range(groups):
        row = within[i : i + 1, :] + total
        result.append(row)
        total = row[:, 127:128]
    return jnp.concatenate(result, axis=1)


def inject_kernel(meta, cells, amounts, out, data, rank_ref, sizes):
    base = (8 * meta[0] - OWN) * 64
    dims = (((1,), (1,)), ((), ()))
    count = cells.shape[1]
    for shot in range(2):
        cell = cells[pl.ds(shot, 1), :]
        row = lax.shift_right_logical(cell, 7) - base - INJECT_FIRST
        inside = jnp.logical_and(row >= 0, row < INJECT_ROWS)
        rank = ordinal(jnp.where(inside, 1.0, 0.0))
        rank_ref[pl.ds(shot, 1), :] = jnp.where(inside, rank, 0.0)
        sizes[shot] = rank[0, count - 1].astype(jnp.int32)
        row = jnp.where(inside, row, 0)
        parts = [
            lax.shift_right_logical(row, 4).astype(jnp.float32),
            jnp.bitwise_and(row, 15).astype(jnp.float32),
            jnp.bitwise_and(cell, 127).astype(jnp.float32),
        ]
        for moment in range(3):
            left = amounts[moment, pl.ds(shot, 1), :]
            for part in range(3):
                piece = left.astype(jnp.bfloat16).astype(jnp.float32)
                left = left - piece
                parts.append(piece)
        parts = parts + [jnp.zeros_like(parts[0])] * 4
        data[shot] = jnp.concatenate(parts, axis=0).astype(jnp.bfloat16)

    for shot in range(2):

        def group(k, carry, first=False):
            wanted = GROUP * k + 1 + lax.broadcasted_iota(jnp.int32, (GROUP, count), 0)
            chosen = wanted.astype(jnp.float32) == rank_ref[pl.ds(shot, 1), :]
            few = lax.dot_general(
                data[shot],
                jnp.where(chosen, 1.0, 0.0).astype(jnp.bfloat16),
                dims,
                preferred_element_type=jnp.float32,
            )
            used = GROUP * k + lax.broadcasted_iota(jnp.int32, (1, GROUP), 1) < sizes[shot]
            row = jnp.where(used, 16.0 * few[0:1, :] + few[1:2, :], -1.0).astype(jnp.int32)
            lane = few[2:3, :].astype(jnp.int32)
            lane_hot = lax.broadcasted_iota(jnp.int32, (128, GROUP), 0) == lane
            values = jnp.concatenate(
                [
                    jnp.where(lane_hot, few[3 + 3 * moment + part : 4 + 3 * moment + part, :], 0.0)
                    for part in range(3)
                    for moment in range(3)
                ],
                axis=0,
            ).astype(jnp.bfloat16)
            size = INJECT_ROWS // 2
            for i in range(2):
                at = i * size + lax.broadcasted_iota(jnp.int32, (size, GROUP), 0)
                total = gathered(
                    jnp.where(at == row, 1.0, 0.0).astype(jnp.bfloat16), values, 3
                )
                place = pl.ds(INJECT_FIRST + i * size, size)
                for moment in range(3):
                    part = total[:, 128 * moment : 128 * moment + 128]

                    if first:
                        out[shot, moment, place, :] = part
                    else:
                        out[shot, moment, place, :] += part

            return carry

        groups = lax.div(sizes[shot] + GROUP - 1, GROUP)
        group(0, 0, True)
        lax.fori_loop(1, groups, group, 0)


def inject(meta, cells, amounts):
    count = cells.shape[1]
    vmem = pl.BlockSpec(memory_space=pltpu.VMEM)
    return pl.pallas_call(
        inject_kernel,
        out_shape=jax.ShapeDtypeStruct((2, 3, SLOTS * 64, 128), jnp.float32),
        in_specs=[pl.BlockSpec(memory_space=pltpu.SMEM), vmem, vmem],
        out_specs=vmem,
        scratch_shapes=[
            pltpu.VMEM((2, 16, count), jnp.bfloat16),
            pltpu.VMEM((2, count), jnp.float32),
            pltpu.SMEM((2,), jnp.int32),
        ],
        compiler_params=pltpu.CompilerParams(vmem_limit_bytes=12 << 20),
        name="receivers",
    )(meta, cells, amounts)


def adjoint_passes(meta, w_both, mats, strains, dense, grads, passes):
    kb = lambda q, flat: -mats[0, q, flat, :]
    slabs = [of_shot(w_both, shot) for shot in range(2)]

    def own(moment, stress, q):
        p = q - OWN
        for begin in range(0, 64, CHUNK):
            flat = pl.ds(begin, CHUNK)
            if moment < 2:
                bulk, shear = grads[0, p, flat, :], grads[1, p, flat, :]
            else:
                bulk, shear = 0.0, 0.0
            for shot, w in enumerate(slabs):
                exx, eyy, ezz, eyz, exz, exy = strain_chunk(w, q, begin)
                fxx, fyy, fzz, fyz, fxz, fxy = [
                    strains[shot, moment, i, p, flat, :] for i in range(6)
                ]
                bulk = bulk + (fxx + fyy + fzz) * (exx + eyy + ezz)
                shear = shear + (
                    2.0 * (fxx * exx + fyy * eyy + fzz * ezz)
                    + (fyz * eyz + fxz * exz + fxy * exy)
                )
                if stress:
                    stress_chunk(w, mats, q, begin, (exx, eyy, ezz, eyz, exz, exy), -1.0)
            grads[0, p, flat, :] = bulk
            grads[1, p, flat, :] = shear

    def outer(q):
        for w in slabs:
            for begin in range(0, 64, CHUNK):
                stress_chunk(w, mats, q, begin, strain_chunk(w, q, begin), -1.0)

    def velocity(moment, q):
        for shot, w in enumerate(slabs):
            velocity_plane(w, kb, q, dense.at[shot, moment])

    def run(i, body):
        even, odd, count = passes[i]
        planes(first_plane(meta, even, odd), count, body)

    run(0, functools.partial(velocity, 2))
    run(1, outer)
    run(2, functools.partial(own, 2, True))
    run(3, functools.partial(velocity, 1))
    run(4, outer)
    run(5, functools.partial(own, 1, True))
    run(6, functools.partial(velocity, 0))
    run(7, functools.partial(own, 0, False))


def give_away(meta, grads, give, passes):
    even, odd, count = passes[7]
    low = first_plane(meta, even, odd) - OWN
    rows = pl.ds(pl.multiple_of(32 - 32 * meta[1], 32), 32)
    for i in range(2):
        for j in range(count):
            give[i, j] = grads[i, low + j, rows, :]


def adjoint_near_kernel(meta, mats, chip, strains, dense, *rest):
    give, grads, *w_both = rest[9:]
    load_chip_halo(meta, chip, w_both, None)
    adjoint_passes(meta, w_both, mats, strains, dense, grads, NEAR)
    give_away(meta, grads, give, NEAR)


def adjoint_far_kernel(meta, cross, mats, strains, dense, *rest):
    give, grads, *w_both = rest[10:]
    load_cross_halo(meta, cross, w_both, None)
    adjoint_passes(meta, w_both, mats, strains, dense, grads, FAR)
    give_away(meta, grads, give, FAR)


def gift(passes):
    return jax.ShapeDtypeStruct((2, passes[7][2], 32, 128), jnp.float32)


def adjoint_near(meta, mats, chip, strains, dense, slabs):
    operands = (meta, mats, chip, strains, dense) + tuple(slabs)
    aliases = {5 + i: 2 + i for i in range(9)}
    out = (gift(NEAR), GRADS) + SLABS
    return call(adjoint_near_kernel, "adjoint_near", operands, out, 1, aliases)


def adjoint_far(meta, cross, mats, strains, dense, held):
    operands = (meta, cross, mats, strains, dense) + tuple(held)
    aliases = {5 + i: 1 + i for i in range(10)}
    out = (gift(FAR), GRADS) + SLABS
    return call(adjoint_far_kernel, "adjoint_far", operands, out, 1, aliases)


def finish_kernel(meta, grads, near, far, out_lambda, out_shear):
    rows = pl.ds(pl.multiple_of(32 * meta[1], 32), 32)
    for ref, passes in ((near, NEAR), (far, FAR)):
        even, odd, count = passes[7]
        low = first_plane(meta, even, odd) - OWN
        for i, out in enumerate((out_lambda, out_shear)):
            for j in range(count):
                out[low + j] = grads[i, low + j, rows, :] + ref[i, j]


def finish(meta, grads, near, far):
    out = jax.ShapeDtypeStruct((8, 32, 128), jnp.float32)
    return call(finish_kernel, "finish", (meta, grads, near, far), (out, out), 1)


def shards(
    lame_lambda, lame_shear, buoyancy, fwd_state, adj_state, src_index, src_amp, recv_index, residual
):
    count = lax.axis_size("space")
    onchip = [(i, i + 1) for i in range(0, count, 2)] + [(i + 1, i) for i in range(0, count, 2)]
    between = [(i, i + 1) for i in range(1, count - 1, 2)]
    between = between + [(j, i) for i, j in between]
    swap_chips = lambda x: lax.ppermute(x, "space", between)
    swap_cores = lambda x: lax.ppermute(x, "space", onchip)
    meta = jnp.stack([lax.axis_index("space"), lax.axis_index("shot")]).astype(jnp.int32)
    mats = (lame_lambda, lame_shear, buoyancy)
    swap_shots = lambda x: lax.ppermute(x, "shot", [(0, 1), (1, 0)])
    amounts = residual.transpose(1, 0, 2)
    f_cross, f_chip, *f_slabs = pack(meta, fwd_state, *mats, None)
    f_cross = swap_chips(f_cross)
    a_cross, a_chip, *a_slabs = pack(meta, adj_state, *mats, (recv_index, amounts))
    a_cross = swap_chips(a_cross)
    f_chip = swap_cores(f_chip)
    dense = inject(meta, recv_index, amounts).reshape(2, 3, SLOTS, 64, 128)
    a_chip = swap_cores(a_chip)
    held = forward_near(meta, src_index, src_amp, *mats, f_chip, f_slabs)
    strains, scaled, *_ = forward_far(meta, src_index, src_amp, f_cross, held)
    near, *held = adjoint_near(meta, scaled, a_chip, strains, dense, a_slabs)
    near = swap_shots(near)
    far, grads, *_ = adjoint_far(meta, a_cross, scaled, strains, dense, held)
    far = swap_shots(far)
    return tuple(finish(meta, grads, near, far))


def solution(mesh):
    in_specs = (
        P("space", None, None),
        P("space", None, None),
        P("space", None, None),
        P(None, "shot", "space", None, None),
        P(None, "shot", "space", None, None),
        P("shot"),
        P("shot", None),
        P("shot", None),
        P("shot", None, None),
    )
    out_specs = (P("space", "shot", None), P("space", "shot", None))
    return jax.shard_map(shards, mesh=mesh, in_specs=in_specs, out_specs=out_specs, check_vma=False)
```
